32 devices in a mesh: tok: 8 (over y, x, core), mdl: 4 (over z).
Axes of the slice: x: 2, y: 2, z: 4, core: 2. Of those that a mesh axis runs over, the one named last changes fastest.
Arguments:
- hidden_states: bfloat16 [4096, 3072], P('tok', 'mdl'), may hold values from -36 to 36
- lengths: int32 [2], replicated, may hold values from 1 to 2277, 3644 in all
- positions: int32 [3, 4096], P(None, 'tok'), may hold values from 0 to 44, as said below
- modulation: float32 [6, 3072], replicated, may hold values from -3 to 3
- query_weight: bfloat16 [3072, 3072], P('tok', 'mdl'), may hold values from -1.1 to 1.1
- key_weight: bfloat16 [3072, 3072], P('tok', 'mdl'), may hold values from -1.1 to 1.1
- value_weight: bfloat16 [3072, 3072], P('tok', 'mdl'), may hold values from -0.109375 to 0.109375
- out_weight: bfloat16 [3072, 3072], P('tok', 'mdl'), may hold values from -0.109375 to 0.109375
- query_gain: float32 [64], replicated, may hold values from 0.1 to 1.9
- key_gain: float32 [64], replicated, may hold values from 0.1 to 1.9
Outputs:
- updated: bfloat16 [4096, 3072], P('tok', 'mdl')
The draws below stay inside these ranges and needn't reach their ends.
Inputs may be any that keep to these rules, and one draw needn't show every extreme that they name: lengths[0] + lengths[1] = 3644, and neither of them exceeds 2277. `positions`: frame below 13, row below 30, column below 45.
All inputs are finite; a program needn't handle non-finite values.
Results may differ from the reference program's by a relative error of at most 0.0045.
Values may be sent and summed in bfloat16 or wider, within the bound.
A program may use at most 128 MiB of HBM per device.

```python
import math
import jax
import jax.numpy as jnp
import numpy as np
from jax import lax

D = 3072
HEADS = 48
HEAD_DIM = 64
TEXT = 226
REQS = 2
TOKENS = 4096
VIDEO = 3644
MOST = 2277


def draw_hidden_states(key, part):
    base_key, row_key, col_key = jax.random.split(jax.random.fold_in(key, 101), 3)
    base = jax.random.truncated_normal(base_key, -4.0, 4.0, (TOKENS, D), jnp.float32)
    row_scale = jnp.exp(jax.random.uniform(row_key, (TOKENS, 1), jnp.float32, math.log(0.3), math.log(3.0)))
    col_scale = jnp.exp(jax.random.uniform(col_key, (1, D), jnp.float32, math.log(0.3), math.log(3.0)))
    return (base * row_scale * col_scale).astype(jnp.bfloat16)


def projection_draw(key, salt):
    base_key, col_key = jax.random.split(jax.random.fold_in(key, salt), 2)
    base = jax.random.truncated_normal(base_key, -4.0, 4.0, (D, D), jnp.float32)
    col_scale = jnp.exp(jax.random.uniform(col_key, (1, D), jnp.float32, math.log(0.3), math.log(3.0)))
    return base * col_scale * D ** (-0.5)


def draw_query_weight(key, part):
    return projection_draw(key, 211).astype(jnp.bfloat16)


def draw_key_weight(key, part):
    return projection_draw(key, 307).astype(jnp.bfloat16)


def draw_positions(key, part):
    limits = jnp.array([[13], [30], [45]], dtype=jnp.int32)
    return jax.random.randint(jax.random.fold_in(key, 7), (3, TOKENS), 0, limits, dtype=jnp.int32)


def levels(key, shape, cuts, smallest, largest):
    factor_of, own = 1.0, jax.random.fold_in(key, 6)
    for position, shards_of in cuts:
        steps = jnp.exp(jax.random.uniform(jax.random.fold_in(own, position), (shards_of,), jnp.float32, smallest / len(cuts), largest / len(cuts)))
        factor_of = factor_of * jnp.repeat(steps, shape[position] // shards_of).reshape([-1 if axis == position else 1 for axis in range(len(shape))])
    return factor_of


def profile(count, total, most, slope):
    weights = [(1 << 20) // math.isqrt(grade ** slope) + 1 for grade in range(2, count + 1)]
    rest, holding = total - most - (count - 1), [1] * (count - 1)
    while rest > 0:
        movable = [i for i in range(count - 1) if holding[i] < most]
        mass, budget = sum([weights[i] for i in movable]), rest
        for i in movable:
            more = min(most - holding[i], max(1, budget * weights[i] // mass), rest)
            holding[i] = holding[i] + more
            rest = rest - more
    return np.array([most] + holding)


def ragged_sizes(rng, amount, total, most, slope):
    if amount == 2:
        one = jax.random.randint(rng, (), max(1, total - most), min(most, total - 1) + 1)
        return jnp.stack([one, total - one])
    sizes = jnp.asarray(profile(amount, total, most, slope), jnp.int32)
    pairs = (amount - 1) // 2
    source_of, sink = sizes[1:1 + 2 * pairs:2], sizes[2:2 + 2 * pairs:2]
    room = jnp.minimum(source_of - 1, most - sink)
    moved = jax.random.randint(jax.random.fold_in(rng, 1), (pairs,), 0, 1 << 20) % (room + 1)
    sizes = sizes.at[1:1 + 2 * pairs:2].set(source_of - moved).at[2:2 + 2 * pairs:2].set(sink + moved)
    return sizes[jax.random.permutation(jax.random.fold_in(rng, 2), amount)]


def bell_draw(rng, dims, scale, limit, shards=(), held_as=jnp.bfloat16):
    drawn = scale * jax.random.normal(rng, dims, jnp.float32)
    if shards:
        drawn = drawn * levels(rng, dims, shards, -0.22, 0.18)
    return jnp.clip(drawn, -limit, limit).astype(held_as)


def setup_inputs(seed: int = 0) -> dict:
    arg_keys = jax.random.split(jax.random.key(seed), 11)
    hidden_states = draw_hidden_states(jax.random.fold_in(arg_keys[10], 71), 0)
    lengths = ragged_sizes(arg_keys[1], REQS, VIDEO, MOST, 0).astype(jnp.int32)
    positions = draw_positions(jax.random.fold_in(arg_keys[10], 71), 0)
    modulation = bell_draw(arg_keys[3], (6, D), 0.5, 3.0, (), jnp.float32)
    query_weight = draw_query_weight(jax.random.fold_in(arg_keys[10], 71), 0)
    key_weight = draw_key_weight(jax.random.fold_in(arg_keys[10], 71), 0)
    value_weight = bell_draw(arg_keys[6], (D, D), D ** -0.5, 0.109375, ((0, 8), (1, 4)))
    out_weight = bell_draw(arg_keys[7], (D, D), D ** -0.5, 0.109375, ((0, 8), (1, 4)))
    query_gain = jnp.clip(1.0 + 0.18 * jax.random.normal(arg_keys[8], (HEAD_DIM,), jnp.float32), 0.1, 1.9)
    key_gain = jnp.clip(1.0 + 0.18 * jax.random.normal(arg_keys[9], (HEAD_DIM,), jnp.float32), 0.1, 1.9)
    return {"hidden_states": hidden_states, "lengths": lengths, "positions": positions, "modulation": modulation, "query_weight": query_weight, "key_weight": key_weight, "value_weight": value_weight, "out_weight": out_weight, "query_gain": query_gain, "key_gain": key_gain}


def token_labels(row_index, lengths):
    bound = TEXT + lengths[0]
    request = (row_index >= bound).astype(jnp.int32)
    place = row_index - request * bound
    return (request, place < TEXT, bound)

def modulate(rows_bf, modulation, is_text):
    values = rows_bf.astype(jnp.float32)
    center = values - lax.optimization_barrier(jnp.mean(values, axis=1, keepdims=True))
    spread = lax.optimization_barrier(jnp.mean(center * center, axis=1, keepdims=True))
    normal = center * lax.rsqrt(spread + 1e-05)
    textual = is_text[:, None]
    shift = jnp.where(textual, modulation[3][None, :], modulation[0][None, :])
    scale = jnp.where(textual, modulation[4][None, :], modulation[1][None, :])
    return (normal * (1.0 + scale) + shift).astype(jnp.bfloat16)

def pair_angles(positions, pairs):
    index = jnp.arange(pairs, dtype=jnp.int32)
    first = pairs // 4
    second = (pairs - first) // 2
    third = pairs - first - second
    component = jnp.where(index < first, 0, jnp.where(index < first + second, 1, 2))
    local = index - jnp.where(component == 0, 0, jnp.where(component == 1, first, first + second))
    count = jnp.where(component == 0, first, jnp.where(component == 1, second, third))
    rates = jnp.power(jnp.float32(10000.0), -local.astype(jnp.float32) / count.astype(jnp.float32))
    places = positions.astype(jnp.float32)
    chosen = jnp.where(component[:, None] == 0, places[0][None, :], jnp.where(component[:, None] == 1, places[1][None, :], places[2][None, :]))
    return jnp.transpose(chosen * rates[:, None])

def head_norm(projected, gain, angles, is_text):
    width = gain.shape[0]
    shaped = projected.reshape(projected.shape[0], -1, width)
    center = shaped - lax.optimization_barrier(jnp.mean(shaped, axis=2, keepdims=True))
    spread = lax.optimization_barrier(jnp.mean(center * center, axis=2, keepdims=True))
    normal = center * lax.rsqrt(spread + 1e-06) * gain
    half = width // 2
    cosine = jnp.cos(angles)[:, None, :]
    sine = jnp.sin(angles)[:, None, :]
    lower = normal[:, :, :half]
    upper = normal[:, :, half:]
    turned = jnp.concatenate([lower * cosine - upper * sine, lower * sine + upper * cosine], axis=2)
    return jnp.where(is_text[:, None, None], normal, turned).astype(jnp.bfloat16)

def reference(hidden_states, lengths, positions, modulation, query_weight, key_weight, value_weight, out_weight, query_gain, key_gain):
    row_index = jnp.arange(TOKENS, dtype=jnp.int32)
    request, is_text, bound = token_labels(row_index, lengths)
    normed = modulate(hidden_states, modulation, is_text)
    angles = pair_angles(positions, HEAD_DIM // 2)
    query = head_norm(jnp.dot(normed, query_weight, preferred_element_type=jnp.float32), query_gain, angles, is_text)
    keys = head_norm(jnp.dot(normed, key_weight, preferred_element_type=jnp.float32), key_gain, angles, is_text)
    values = jnp.dot(normed, value_weight, preferred_element_type=jnp.float32).astype(jnp.bfloat16)
    values = values.reshape(TOKENS, HEADS, HEAD_DIM)
    same = request[:, None] == request[None, :]
    factor = HEAD_DIM ** (-0.5)

    def one_head(operands):
        head_query, head_keys, head_values = operands
        score = jnp.dot(head_query, jnp.transpose(head_keys), preferred_element_type=jnp.float32) * factor
        expo = jnp.where(same, jnp.exp(score), jnp.float32(0.0))
        total = lax.optimization_barrier(jnp.sum(expo, axis=1, keepdims=True))
        weighted = jnp.dot(expo.astype(jnp.bfloat16), head_values, preferred_element_type=jnp.float32)
        return weighted / total
    heads_out = lax.map(one_head, (jnp.transpose(query, (1, 0, 2)), jnp.transpose(keys, (1, 0, 2)), jnp.transpose(values, (1, 0, 2))))
    attended = jnp.transpose(heads_out, (1, 0, 2)).reshape(TOKENS, D).astype(jnp.bfloat16)
    projected = jnp.dot(attended, out_weight, preferred_element_type=jnp.float32)
    gate = jnp.where(is_text[:, None], modulation[5][None, :], modulation[2][None, :])
    return (hidden_states.astype(jnp.float32) + gate * projected).astype(jnp.bfloat16)
```

```python
import functools
import jax
import jax.numpy as jnp
from jax import lax
from jax.experimental import pallas as pl
from jax.experimental.pallas import tpu as pltpu
from jax.sharding import PartitionSpec as P

TEXT = 226


def token_labels(row_index, lengths):
    bound = TEXT + lengths[0]
    request = (row_index >= bound).astype(jnp.int32)
    place = row_index - request * bound
    return (request, place < TEXT, bound)


def modulate(rows_bf, modulation, is_text):
    values = rows_bf.astype(jnp.float32)
    center = values - jnp.mean(values, axis=1, keepdims=True)
    spread = jnp.mean(center * center, axis=1, keepdims=True)
    normal = center * lax.rsqrt(spread + 1e-05)
    textual = is_text[:, None]
    shift = jnp.where(textual, modulation[3][None, :], modulation[0][None, :])
    scale = jnp.where(textual, modulation[4][None, :], modulation[1][None, :])
    return (normal * (1.0 + scale) + shift).astype(jnp.bfloat16)


def pair_angles(positions, pairs):
    index = jnp.arange(pairs, dtype=jnp.int32)
    first = pairs // 4
    second = (pairs - first) // 2
    third = pairs - first - second
    component = jnp.where(index < first, 0, jnp.where(index < first + second, 1, 2))
    local = index - jnp.where(component == 0, 0, jnp.where(component == 1, first, first + second))
    count = jnp.where(component == 0, first, jnp.where(component == 1, second, third))
    rates = jnp.power(jnp.float32(10000.0), -local.astype(jnp.float32) / count.astype(jnp.float32))
    places = positions.astype(jnp.float32)
    chosen = jnp.where(
        component[:, None] == 0,
        places[0][None, :],
        jnp.where(component[:, None] == 1, places[1][None, :], places[2][None, :]),
    )
    return jnp.transpose(chosen * rates[:, None])


def head_norm(projected, gain, angles, is_text):
    width = gain.shape[0]
    shaped = projected.reshape(projected.shape[0], -1, width)
    center = shaped - jnp.mean(shaped, axis=2, keepdims=True)
    spread = jnp.mean(center * center, axis=2, keepdims=True)
    normal = center * lax.rsqrt(spread + 1e-06) * gain
    half = width // 2
    cosine = jnp.cos(angles)[:, None, :]
    sine = jnp.sin(angles)[:, None, :]
    lower = normal[:, :, :half]
    upper = normal[:, :, half:]
    turned = jnp.concatenate([lower * cosine - upper * sine, lower * sine + upper * cosine], axis=2)
    return jnp.where(is_text[:, None, None], normal, turned).astype(jnp.bfloat16)


def gather_kernel(n_tok, n_mdl, n_row, n_col, *refs):
    rows_in = refs[:n_row]
    cols_in = refs[n_row : n_row + n_col]
    outs = refs[n_row + n_col : 2 * (n_row + n_col)]
    rows_out, cols_out = outs[:n_row], outs[n_row:]
    local_sem, send1, recv1, send2, recv2, to_right, from_left, to_left, from_right = refs[
        2 * (n_row + n_col) :
    ]
    chips = n_tok // 2
    tok, mdl = lax.axis_index("tok"), lax.axis_index("mdl")
    chip, core = tok // 2, tok % 2
    sibling = chip * 2 + 1 - core

    def chip_at(step):
        return (chip + step) % chips

    barrier = pltpu.get_barrier_semaphore()
    greeted = 0
    if n_row:
        for step in range(1, chips):
            pl.semaphore_signal(
                barrier, inc=1, device_id={"tok": chip_at(step) * 2 + core, "mdl": mdl}
            )
            greeted += 1
        pl.semaphore_signal(barrier, inc=1, device_id={"tok": sibling, "mdl": mdl})
        greeted += 1
    if n_col:
        for side in (1, n_mdl - 1):
            pl.semaphore_signal(
                barrier, inc=1, device_id={"tok": tok, "mdl": (mdl + side) % n_mdl}
            )
            greeted += 1
    pl.semaphore_wait(barrier, greeted)

    def row_block(number, owner):
        size = rows_in[number].shape[0]
        return rows_out[number].at[pl.ds(pl.multiple_of(owner * size, size), size), :]

    def col_block(number, owner):
        size = cols_in[number].shape[1]
        return cols_out[number].at[:, pl.ds(pl.multiple_of(owner * size, size), size)]

    def direct(number, step):
        target = chip_at(step) * 2 + core if step else sibling
        return pltpu.make_async_remote_copy(
            src_ref=rows_in[number],
            dst_ref=row_block(number, tok),
            send_sem=send1.at[number, step],
            recv_sem=recv1.at[number, step],
            device_id={"tok": target, "mdl": mdl},
        )

    def passed(number, step):
        block = row_block(number, chip_at(chips - step) * 2 + core)
        return pltpu.make_async_remote_copy(
            src_ref=block,
            dst_ref=block,
            send_sem=send2.at[number, step],
            recv_sem=recv2.at[number, step],
            device_id={"tok": sibling, "mdl": mdl},
        )

    def rightward(number, step):
        block = col_block(number, mdl - step)
        return pltpu.make_async_remote_copy(
            src_ref=block if step else cols_in[number],
            dst_ref=block,
            send_sem=to_right.at[number, step],
            recv_sem=from_left.at[number, step],
            device_id={"tok": tok, "mdl": mdl + 1},
        )

    def leftward(number, step):
        block = col_block(number, mdl + step)
        return pltpu.make_async_remote_copy(
            src_ref=block if step else cols_in[number],
            dst_ref=block,
            send_sem=to_left.at[number, step],
            recv_sem=from_right.at[number, step],
            device_id={"tok": tok, "mdl": mdl - 1},
        )

    def right_if(step):
        return (mdl >= step) & (mdl < n_mdl - 1)

    def left_if(step):
        return (mdl + step < n_mdl) & (mdl > 0)

    for number in range(n_col):
        @pl.when(right_if(0))
        def _():
            rightward(number, 0).start()

        @pl.when(left_if(0))
        def _():
            leftward(number, 0).start()

    for number in range(n_row):
        for step in range(1, chips):
            direct(number, step).start()
        direct(number, 0).start()
    locals_ = []
    for number in range(n_row):
        locals_.append(
            pltpu.make_async_copy(rows_in[number], row_block(number, tok), local_sem.at[number])
        )
    for number in range(n_col):
        locals_.append(
            pltpu.make_async_copy(
                cols_in[number], col_block(number, mdl), local_sem.at[n_row + number]
            )
        )
    for copy in locals_:
        copy.start()

    for turn in range(max(n_row, n_mdl - 1 if n_col else 0)):
        hop = turn + 1
        if hop < n_mdl:
            for number in range(n_col):
                @pl.when(mdl >= hop)
                def _():
                    rightward(number, hop - 1).wait_recv()

                @pl.when(right_if(hop))
                def _():
                    rightward(number, hop).start()

                @pl.when(mdl + hop < n_mdl)
                def _():
                    leftward(number, hop - 1).wait_recv()

                @pl.when(left_if(hop))
                def _():
                    leftward(number, hop).start()

        if turn < n_row:
            for step in range(1, chips):
                direct(turn, step).wait_recv()
                passed(turn, step).start()

    for copy in locals_:
        copy.wait()
    for number in range(n_row):
        for step in range(chips):
            direct(number, step).wait_send()
            if step:
                passed(number, step).wait()
            else:
                direct(number, step).wait_recv()
    for number in range(n_col):
        for step in range(n_mdl - 1):
            @pl.when(right_if(step))
            def _():
                rightward(number, step).wait_send()

            @pl.when(left_if(step))
            def _():
                leftward(number, step).wait_send()


def gather_all(mesh, over_tok, over_mdl, collective_id):
    n_tok, n_mdl = mesh.shape["tok"], mesh.shape["mdl"]
    n_row, n_col = len(over_tok), len(over_mdl)
    shapes = [
        jax.ShapeDtypeStruct((one.shape[0] * n_tok, one.shape[1]), one.dtype) for one in over_tok
    ] + [jax.ShapeDtypeStruct((one.shape[0], one.shape[1] * n_mdl), one.dtype) for one in over_mdl]
    chips = n_tok // 2
    row_sem = pltpu.SemaphoreType.DMA((max(n_row, 1), chips))
    col_sem = pltpu.SemaphoreType.DMA((max(n_col, 1), n_mdl))
    return pl.pallas_call(
        functools.partial(gather_kernel, n_tok, n_mdl, n_row, n_col),
        out_shape=shapes,
        in_specs=[pl.BlockSpec(memory_space=pl.ANY)] * (n_row + n_col),
        out_specs=[pl.BlockSpec(memory_space=pl.ANY)] * (n_row + n_col),
        scratch_shapes=[pltpu.SemaphoreType.DMA((n_row + n_col,))] + [row_sem] * 4 + [col_sem] * 4,
        compiler_params=pltpu.CompilerParams(collective_id=collective_id, has_side_effects=True),
        name=f"gather_{collective_id}",
    )(*over_tok, *over_mdl)


def attend_kernel(rows_at_once, keys_at_once, head_width, meta_ref, q_ref, k_ref, v_ref, o_ref):
    bound, first_row = meta_ref[0], meta_ref[1]
    own_rows, lanes = q_ref.shape
    count = k_ref.shape[0]
    chunks = count // keys_at_once
    per = lanes // head_width
    lane = lax.broadcasted_iota(jnp.int32, (1, lanes), 1) // head_width
    masks = [(lane == head).astype(jnp.float32) for head in range(per)]
    edge = bound // keys_at_once
    edge_start = pl.multiple_of(edge * keys_at_once, keys_at_once)
    edge_keys = edge_start + lax.broadcasted_iota(jnp.int32, (keys_at_once, 1), 0)

    for block in range(own_rows // rows_at_once):
        rows = pl.ds(block * rows_at_once, rows_at_once)
        start = first_row + block * rows_at_once
        row_ids = start + lax.broadcasted_iota(jnp.int32, (rows_at_once, 1), 0)

        def add_chunk(carry, keys, values):
            queries = q_ref[rows, :]
            result = []
            for head in range(per):
                mine = queries * (masks[head] * head_width ** (-0.5)).astype(jnp.bfloat16)
                score = lax.dot_general(
                    mine, keys, (((1,), (1,)), ((), ())), preferred_element_type=jnp.float32
                )
                expo = jnp.exp(score).astype(jnp.bfloat16)
                result.append(
                    carry[head]
                    + jnp.dot(expo, values[head], preferred_element_type=jnp.float32)
                )
            return tuple(result)

        def inner(chunk, carry):
            here = pl.ds(pl.multiple_of(chunk * keys_at_once, keys_at_once), keys_at_once)
            values = v_ref[here, :]
            with_ones = [
                values * mask.astype(jnp.bfloat16) + (1.0 - mask).astype(jnp.bfloat16)
                for mask in masks
            ]
            return add_chunk(carry, k_ref[here, :], with_ones)

        for request in range(2):
            active = start < bound if request == 0 else start + rows_at_once > bound

            @pl.when(active)
            def _():
                here = pl.ds(edge_start, keys_at_once)
                inside = edge_keys < bound if request == 0 else edge_keys >= bound
                wide = v_ref[here, :].astype(jnp.float32)
                with_ones = [
                    jnp.where(inside, wide * mask + (1.0 - mask), 0.0).astype(jnp.bfloat16)
                    for mask in masks
                ]
                zero = jnp.zeros((rows_at_once, lanes), jnp.float32)
                carry = add_chunk((zero,) * per, k_ref[here, :], with_ones)
                if request == 0:
                    low, high = 0, edge
                else:
                    low, high = edge + 1, chunks
                carry = lax.fori_loop(low, high, inner, carry)
                output = zero
                for head in range(per):
                    total = pltpu.roll(carry[head], head_width, axis=1)
                    output = jnp.where(lane == head, carry[head] / total, output)
                if request == 0:
                    o_ref[rows, :] = output.astype(o_ref.dtype)
                else:
                    old = o_ref[rows, :].astype(jnp.float32)
                    o_ref[rows, :] = jnp.where(row_ids >= bound, output, old).astype(o_ref.dtype)


def attend(query, keys, values, bound, first_row, head_width):
    own_rows, width = query.shape
    count = keys.shape[0]
    lanes = 2 * head_width
    meta = jnp.stack([bound, first_row]).astype(jnp.int32)
    block = pl.BlockSpec((own_rows, lanes), lambda pair, meta: (0, pair))
    full = pl.BlockSpec((count, lanes), lambda pair, meta: (0, pair))
    return pl.pallas_call(
        functools.partial(attend_kernel, 256, 512, head_width),
        out_shape=jax.ShapeDtypeStruct((own_rows, width), jnp.bfloat16),
        grid_spec=pltpu.PrefetchScalarGridSpec(
            num_scalar_prefetch=1,
            grid=(width // lanes,),
            in_specs=[block, full, full],
            out_specs=block,
        ),
        compiler_params=pltpu.CompilerParams(vmem_limit_bytes=40 * 2**20),
        cost_estimate=pl.CostEstimate(
            flops=4 * own_rows * count * width,
            bytes_accessed=4 * count * width,
            transcendentals=own_rows * count * width // head_width,
        ),
        name="attend",
    )(meta, query, keys, values)


def shards(
    mesh,
    hidden_states,
    lengths,
    positions,
    modulation,
    query_weight,
    key_weight,
    value_weight,
    out_weight,
    query_gain,
    key_gain,
):
    own_rows = hidden_states.shape[0]
    local_width = query_weight.shape[1]
    head_width = query_gain.shape[0]
    local_heads = local_width // head_width
    key_full, value_full, query_full, full_rows = gather_all(
        mesh, [key_weight, value_weight, query_weight], [hidden_states], 0
    )
    row_index = lax.axis_index("tok") * own_rows + jnp.arange(own_rows, dtype=jnp.int32)
    request, is_text, bound = token_labels(row_index, lengths)
    normed = modulate(full_rows, modulation, is_text)
    angles = pair_angles(positions, head_width // 2)
    pieces = (query_full, key_full, value_full)
    columns = normed
    query_sum, key_sum, value_sum = tuple(
        (
            jnp.dot(columns, pieces[number], preferred_element_type=jnp.float32)
            for number in range(3)
        )
    )
    query = head_norm(query_sum, query_gain, angles, is_text)
    key_flat = head_norm(key_sum, key_gain, angles, is_text).reshape(own_rows, local_width)
    value_flat = value_sum.astype(jnp.bfloat16)
    keys, values = gather_all(mesh, [key_flat, value_flat], [], 1)
    attended = attend(
        query.reshape(own_rows, local_width),
        keys,
        values,
        bound,
        lax.axis_index("tok") * own_rows,
        head_width,
    )
    out_full, all_heads = gather_all(mesh, [out_weight], [attended], 2)
    out_width = out_weight.shape[1]
    projected = jnp.dot(all_heads, out_full, preferred_element_type=jnp.float32)
    gate_rows = lax.dynamic_slice_in_dim(
        modulation, lax.axis_index("mdl") * out_width, out_width, 1
    )
    gate = jnp.where(is_text[:, None], gate_rows[5][None, :], gate_rows[2][None, :])
    return (hidden_states.astype(jnp.float32) + gate * projected).astype(jnp.bfloat16)


def solution(mesh):
    return jax.shard_map(
        functools.partial(shards, mesh),
        mesh=mesh,
        in_specs=(
            P("tok", "mdl"),
            P(),
            P(None, "tok"),
            P(),
            P("tok", "mdl"),
            P("tok", "mdl"),
            P("tok", "mdl"),
            P("tok", "mdl"),
            P(),
            P(),
        ),
        out_specs=P("tok", "mdl"),
        check_vma=False,
    )
```

```python
import functools
import jax
import jax.numpy as jnp
from jax import lax
from jax.experimental import pallas as pl
from jax.experimental.pallas import tpu as pltpu
from jax.sharding import PartitionSpec as P

TEXT = 226


def token_labels(row_index, lengths):
    bound = TEXT + lengths[0]
    request = (row_index >= bound).astype(jnp.int32)
    place = row_index - request * bound
    return (request, place < TEXT, bound)


def modulate(rows_bf, modulation, is_text):
    values = rows_bf.astype(jnp.float32)
    center = values - jnp.mean(values, axis=1, keepdims=True)
    spread = jnp.mean(center * center, axis=1, keepdims=True)
    normal = center * lax.rsqrt(spread + 1e-05)
    textual = is_text[:, None]
    shift = jnp.where(textual, modulation[3][None, :], modulation[0][None, :])
    scale = jnp.where(textual, modulation[4][None, :], modulation[1][None, :])
    return (normal * (1.0 + scale) + shift).astype(jnp.bfloat16)


def pair_angles(positions, pairs):
    index = jnp.arange(pairs, dtype=jnp.int32)
    first = pairs // 4
    second = (pairs - first) // 2
    third = pairs - first - second
    component = jnp.where(index < first, 0, jnp.where(index < first + second, 1, 2))
    local = index - jnp.where(component == 0, 0, jnp.where(component == 1, first, first + second))
    count = jnp.where(component == 0, first, jnp.where(component == 1, second, third))
    rates = jnp.power(jnp.float32(10000.0), -local.astype(jnp.float32) / count.astype(jnp.float32))
    places = positions.astype(jnp.float32)
    chosen = jnp.where(
        component[:, None] == 0,
        places[0][None, :],
        jnp.where(component[:, None] == 1, places[1][None, :], places[2][None, :]),
    )
    return jnp.transpose(chosen * rates[:, None])


def head_norm(projected, gain, angles, is_text):
    width = gain.shape[0]
    shaped = projected.reshape(projected.shape[0], -1, width)
    center = shaped - jnp.mean(shaped, axis=2, keepdims=True)
    spread = jnp.mean(center * center, axis=2, keepdims=True)
    normal = center * lax.rsqrt(spread + 1e-06) * gain
    half = width // 2
    cosine = jnp.cos(angles)[:, None, :]
    sine = jnp.sin(angles)[:, None, :]
    lower = normal[:, :, :half]
    upper = normal[:, :, half:]
    turned = jnp.concatenate([lower * cosine - upper * sine, lower * sine + upper * cosine], axis=2)
    return jnp.where(is_text[:, None, None], normal, turned).astype(jnp.bfloat16)


def gather_kernel(n_tok, n_mdl, n_row, n_col, *refs):
    rows_in = refs[:n_row]
    cols_in = refs[n_row : n_row + n_col]
    outs = refs[n_row + n_col : 2 * (n_row + n_col)]
    rows_out, cols_out = outs[:n_row], outs[n_row:]
    (
        local_sem,
        send1,
        recv1,
        send2,
        recv2,
        send3,
        recv3,
        to_right,
        from_left,
        to_left,
        from_right,
    ) = refs[2 * (n_row + n_col) :]
    square = n_tok == 8
    chips = n_tok // 2
    tok, mdl = lax.axis_index("tok"), lax.axis_index("mdl")
    chip, core = tok // 2, tok % 2
    sibling = chip * 2 + 1 - core

    def chip_at(step):
        if square:
            return (chip, chip + 1 - 2 * (chip % 2), (chip + 2) % 4, 3 - chip)[step]
        return (chip + step) % chips

    def source_at(step):
        return chip_at(step) if square else chip_at(chips - step)

    barrier = pltpu.get_barrier_semaphore()
    greeted = 0
    if n_row:
        for step in (1, 2) if square else range(1, chips):
            pl.semaphore_signal(
                barrier, inc=1, device_id={"tok": chip_at(step) * 2 + core, "mdl": mdl}
            )
            greeted += 1
        pl.semaphore_signal(barrier, inc=1, device_id={"tok": sibling, "mdl": mdl})
        greeted += 1
    if n_col:
        for side in (1, n_mdl - 1):
            pl.semaphore_signal(
                barrier, inc=1, device_id={"tok": tok, "mdl": (mdl + side) % n_mdl}
            )
            greeted += 1
    pl.semaphore_wait(barrier, greeted)

    def row_block(number, owner):
        size = rows_in[number].shape[0]
        return rows_out[number].at[pl.ds(pl.multiple_of(owner * size, size), size), :]

    def col_block(number, owner):
        size = cols_in[number].shape[1]
        return cols_out[number].at[:, pl.ds(pl.multiple_of(owner * size, size), size)]

    def direct(number, step):
        target = chip_at(step) * 2 + core if step else sibling
        return pltpu.make_async_remote_copy(
            src_ref=rows_in[number],
            dst_ref=row_block(number, tok),
            send_sem=send1.at[number, step],
            recv_sem=recv1.at[number, step],
            device_id={"tok": target, "mdl": mdl},
        )

    def passed(number, step):
        block = row_block(number, source_at(step) * 2 + core)
        return pltpu.make_async_remote_copy(
            src_ref=block,
            dst_ref=block,
            send_sem=send2.at[number, step],
            recv_sem=recv2.at[number, step],
            device_id={"tok": sibling, "mdl": mdl},
        )

    def relayed(number, step):
        half = rows_in[number].shape[0] // 2
        first = (source_at(step) * 2 + core) * 2 * half + (step - 1) * half
        block = rows_out[number].at[pl.ds(pl.multiple_of(first, half), half), :]
        return pltpu.make_async_remote_copy(
            src_ref=block,
            dst_ref=block,
            send_sem=send3.at[number, step],
            recv_sem=recv3.at[number, step],
            device_id={"tok": chip_at(3 - step) * 2 + core, "mdl": mdl},
        )

    directs = (1, 2) if square else range(1, chips)

    def rightward(number, step):
        block = col_block(number, mdl - step)
        return pltpu.make_async_remote_copy(
            src_ref=block if step else cols_in[number],
            dst_ref=block,
            send_sem=to_right.at[number, step],
            recv_sem=from_left.at[number, step],
            device_id={"tok": tok, "mdl": mdl + 1},
        )

    def leftward(number, step):
        block = col_block(number, mdl + step)
        return pltpu.make_async_remote_copy(
            src_ref=block if step else cols_in[number],
            dst_ref=block,
            send_sem=to_left.at[number, step],
            recv_sem=from_right.at[number, step],
            device_id={"tok": tok, "mdl": mdl - 1},
        )

    def right_if(step):
        return (mdl >= step) & (mdl < n_mdl - 1)

    def left_if(step):
        return (mdl + step < n_mdl) & (mdl > 0)

    for number in range(n_col):
        @pl.when(right_if(0))
        def _():
            rightward(number, 0).start()

        @pl.when(left_if(0))
        def _():
            leftward(number, 0).start()

    for number in range(n_row):
        for step in directs:
            direct(number, step).start()
        direct(number, 0).start()
    locals_ = []
    for number in range(n_row):
        locals_.append(
            pltpu.make_async_copy(rows_in[number], row_block(number, tok), local_sem.at[number])
        )
    for number in range(n_col):
        locals_.append(
            pltpu.make_async_copy(
                cols_in[number], col_block(number, mdl), local_sem.at[n_row + number]
            )
        )
    for copy in locals_:
        copy.start()

    def finish_diagonal(number):
        for step in (1, 2):
            relayed(number, step).wait_recv()
        passed(number, 3).start()

    for turn in range(max(n_row, n_mdl - 1 if n_col else 0)):
        hop = turn + 1
        if hop < n_mdl:
            for number in range(n_col):
                @pl.when(mdl >= hop)
                def _():
                    rightward(number, hop - 1).wait_recv()

                @pl.when(right_if(hop))
                def _():
                    rightward(number, hop).start()

                @pl.when(mdl + hop < n_mdl)
                def _():
                    leftward(number, hop - 1).wait_recv()

                @pl.when(left_if(hop))
                def _():
                    leftward(number, hop).start()

        if turn < n_row:
            for step in directs:
                direct(turn, step).wait_recv()
                if square:
                    relayed(turn, step).start()
                passed(turn, step).start()
            if square and turn > 0:
                finish_diagonal(turn - 1)

    if square and n_row:
        finish_diagonal(n_row - 1)
    for copy in locals_:
        copy.wait()
    for number in range(n_row):
        direct(number, 0).wait()
        for step in directs:
            direct(number, step).wait_send()
            if square:
                relayed(number, step).wait_send()
        for step in range(1, chips):
            passed(number, step).wait()
    for number in range(n_col):
        for step in range(n_mdl - 1):
            @pl.when(right_if(step))
            def _():
                rightward(number, step).wait_send()

            @pl.when(left_if(step))
            def _():
                leftward(number, step).wait_send()


def gather_all(mesh, over_tok, over_mdl, collective_id):
    n_tok, n_mdl = mesh.shape["tok"], mesh.shape["mdl"]
    n_row, n_col = len(over_tok), len(over_mdl)
    shapes = [
        jax.ShapeDtypeStruct((one.shape[0] * n_tok, one.shape[1]), one.dtype) for one in over_tok
    ] + [jax.ShapeDtypeStruct((one.shape[0], one.shape[1] * n_mdl), one.dtype) for one in over_mdl]
    chips = n_tok // 2
    row_sem = pltpu.SemaphoreType.DMA((max(n_row, 1), chips))
    col_sem = pltpu.SemaphoreType.DMA((max(n_col, 1), n_mdl))
    return pl.pallas_call(
        functools.partial(gather_kernel, n_tok, n_mdl, n_row, n_col),
        out_shape=shapes,
        in_specs=[pl.BlockSpec(memory_space=pl.ANY)] * (n_row + n_col),
        out_specs=[pl.BlockSpec(memory_space=pl.ANY)] * (n_row + n_col),
        scratch_shapes=[pltpu.SemaphoreType.DMA((n_row + n_col,))] + [row_sem] * 6 + [col_sem] * 4,
        compiler_params=pltpu.CompilerParams(collective_id=collective_id, has_side_effects=True),
        name=f"gather_{collective_id}",
    )(*over_tok, *over_mdl)


def attend_kernel(rows_at_once, keys_at_once, head_width, meta_ref, q_ref, k_ref, v_ref, o_ref):
    bound, first_row = meta_ref[0], meta_ref[1]
    own_rows, lanes = q_ref.shape
    count = k_ref.shape[0]
    chunks = count // keys_at_once
    per = lanes // head_width
    lane = lax.broadcasted_iota(jnp.int32, (1, lanes), 1) // head_width
    masks = [(lane == head).astype(jnp.float32) for head in range(per)]
    edge = bound // keys_at_once
    edge_start = pl.multiple_of(edge * keys_at_once, keys_at_once)
    edge_keys = edge_start + lax.broadcasted_iota(jnp.int32, (keys_at_once, 1), 0)

    for block in range(own_rows // rows_at_once):
        rows = pl.ds(block * rows_at_once, rows_at_once)
        start = first_row + block * rows_at_once
        row_ids = start + lax.broadcasted_iota(jnp.int32, (rows_at_once, 1), 0)

        def add_chunk(carry, keys, values):
            queries = q_ref[rows, :]
            result = []
            for head in range(per):
                mine = queries * (masks[head] * head_width ** (-0.5)).astype(jnp.bfloat16)
                score = lax.dot_general(
                    mine, keys, (((1,), (1,)), ((), ())), preferred_element_type=jnp.float32
                )
                expo = jnp.exp(score).astype(jnp.bfloat16)
                result.append(
                    carry[head]
                    + jnp.dot(expo, values[head], preferred_element_type=jnp.float32)
                )
            return tuple(result)

        def inner(chunk, carry):
            here = pl.ds(pl.multiple_of(chunk * keys_at_once, keys_at_once), keys_at_once)
            values = v_ref[here, :]
            with_ones = [
                values * mask.astype(jnp.bfloat16) + (1.0 - mask).astype(jnp.bfloat16)
                for mask in masks
            ]
            return add_chunk(carry, k_ref[here, :], with_ones)

        for request in range(2):
            active = start < bound if request == 0 else start + rows_at_once > bound

            @pl.when(active)
            def _():
                here = pl.ds(edge_start, keys_at_once)
                inside = edge_keys < bound if request == 0 else edge_keys >= bound
                wide = v_ref[here, :].astype(jnp.float32)
                with_ones = [
                    jnp.where(inside, wide * mask + (1.0 - mask), 0.0).astype(jnp.bfloat16)
                    for mask in masks
                ]
                zero = jnp.zeros((rows_at_once, lanes), jnp.float32)
                carry = add_chunk((zero,) * per, k_ref[here, :], with_ones)
                if request == 0:
                    low, high = 0, edge
                else:
                    low, high = edge + 1, chunks
                carry = lax.fori_loop(low, high, inner, carry)
                output = zero
                for head in range(per):
                    total = pltpu.roll(carry[head], head_width, axis=1)
                    output = jnp.where(lane == head, carry[head] / total, output)
                if request == 0:
                    o_ref[rows, :] = output.astype(o_ref.dtype)
                else:
                    old = o_ref[rows, :].astype(jnp.float32)
                    o_ref[rows, :] = jnp.where(row_ids >= bound, output, old).astype(o_ref.dtype)


def attend(query, keys, values, bound, first_row, head_width, part, parts):
    width = query.shape[1]
    own_rows = query.shape[0] // parts
    count = keys.shape[0]
    lanes = 2 * head_width
    meta = jnp.stack([bound, first_row + part * own_rows]).astype(jnp.int32)
    block = pl.BlockSpec((own_rows, lanes), lambda pair, meta: (part, pair))
    out_block = pl.BlockSpec((own_rows, lanes), lambda pair, meta: (0, pair))
    full = pl.BlockSpec((count, lanes), lambda pair, meta: (0, pair))
    return pl.pallas_call(
        functools.partial(attend_kernel, 256, 512, head_width),
        out_shape=jax.ShapeDtypeStruct((own_rows, width), jnp.bfloat16),
        grid_spec=pltpu.PrefetchScalarGridSpec(
            num_scalar_prefetch=1,
            grid=(width // lanes,),
            in_specs=[block, full, full],
            out_specs=out_block,
        ),
        compiler_params=pltpu.CompilerParams(vmem_limit_bytes=58 * 2**20),
        cost_estimate=pl.CostEstimate(
            flops=4 * own_rows * count * width,
            bytes_accessed=4 * count * width,
            transcendentals=own_rows * count * width // head_width,
        ),
        name=f"attend_{part}",
    )(meta, query, keys, values)


def shards(
    mesh,
    hidden_states,
    lengths,
    positions,
    modulation,
    query_weight,
    key_weight,
    value_weight,
    out_weight,
    query_gain,
    key_gain,
):
    own_rows = hidden_states.shape[0]
    local_width = query_weight.shape[1]
    head_width = query_gain.shape[0]
    local_heads = local_width // head_width
    key_full, value_full, query_full, full_rows = gather_all(
        mesh, [key_weight, value_weight, query_weight], [hidden_states], 0
    )
    row_index = lax.axis_index("tok") * own_rows + jnp.arange(own_rows, dtype=jnp.int32)
    request, is_text, bound = token_labels(row_index, lengths)
    normed = modulate(full_rows, modulation, is_text)
    angles = pair_angles(positions, head_width // 2)
    pieces = (query_full, key_full, value_full)
    columns = normed
    query_sum, key_sum, value_sum = tuple(
        (
            jnp.dot(columns, pieces[number], preferred_element_type=jnp.float32)
            for number in range(3)
        )
    )
    query = head_norm(query_sum, query_gain, angles, is_text)
    key_flat = head_norm(key_sum, key_gain, angles, is_text).reshape(own_rows, local_width)
    value_flat = value_sum.astype(jnp.bfloat16)
    keys, values = gather_all(mesh, [key_flat, value_flat], [], 1)
    query_flat = query.reshape(own_rows, local_width)
    first_row = lax.axis_index("tok") * own_rows
    first, second = (
        attend(query_flat, keys, values, bound, first_row, head_width, part, 2)
        for part in range(2)
    )
    first_heads = lax.all_gather(first, "mdl", axis=1, tiled=True)
    out_full, second_heads = gather_all(mesh, [out_weight], [second], 2)
    out_width = out_weight.shape[1]
    projected = jnp.concatenate(
        [
            jnp.dot(heads, out_full, preferred_element_type=jnp.float32)
            for heads in (first_heads, second_heads)
        ],
        axis=0,
    )
    gate_rows = lax.dynamic_slice_in_dim(
        modulation, lax.axis_index("mdl") * out_width, out_width, 1
    )
    gate = jnp.where(is_text[:, None], gate_rows[5][None, :], gate_rows[2][None, :])
    return (hidden_states.astype(jnp.float32) + gate * projected).astype(jnp.bfloat16)


def solution(mesh):
    return jax.shard_map(
        functools.partial(shards, mesh),
        mesh=mesh,
        in_specs=(
            P("tok", "mdl"),
            P(),
            P(None, "tok"),
            P(),
            P("tok", "mdl"),
            P("tok", "mdl"),
            P("tok", "mdl"),
            P("tok", "mdl"),
            P(),
            P(),
        ),
        out_specs=P("tok", "mdl"),
        check_vma=False,
    )
```

```python
import functools
import jax
import jax.numpy as jnp
from jax import lax
from jax.experimental import pallas as pl
from jax.experimental.pallas import tpu as pltpu
from jax.sharding import PartitionSpec as P

TEXT = 226


def token_labels(row_index, lengths):
    bound = TEXT + lengths[0]
    request = (row_index >= bound).astype(jnp.int32)
    place = row_index - request * bound
    return (request, place < TEXT, bound)


def modulate(rows_bf, modulation, is_text):
    values = rows_bf.astype(jnp.float32)
    center = values - jnp.mean(values, axis=1, keepdims=True)
    spread = jnp.mean(center * center, axis=1, keepdims=True)
    normal = center * lax.rsqrt(spread + 1e-05)
    textual = is_text[:, None]
    shift = jnp.where(textual, modulation[3][None, :], modulation[0][None, :])
    scale = jnp.where(textual, modulation[4][None, :], modulation[1][None, :])
    return (normal * (1.0 + scale) + shift).astype(jnp.bfloat16)


def pair_angles(positions, pairs):
    index = jnp.arange(pairs, dtype=jnp.int32)
    first = pairs // 4
    second = (pairs - first) // 2
    third = pairs - first - second
    component = jnp.where(index < first, 0, jnp.where(index < first + second, 1, 2))
    local = index - jnp.where(component == 0, 0, jnp.where(component == 1, first, first + second))
    count = jnp.where(component == 0, first, jnp.where(component == 1, second, third))
    rates = jnp.power(jnp.float32(10000.0), -local.astype(jnp.float32) / count.astype(jnp.float32))
    places = positions.astype(jnp.float32)
    chosen = jnp.where(
        component[:, None] == 0,
        places[0][None, :],
        jnp.where(component[:, None] == 1, places[1][None, :], places[2][None, :]),
    )
    return jnp.transpose(chosen * rates[:, None])


def gather_kernel(n_tok, n_mdl, n_row, n_col, *refs):
    count = n_row + n_col
    ins, outs = refs[:count], refs[count : 2 * count]
    exchange(
        n_tok, n_mdl, ins[:n_row], ins[n_row:], outs[:n_row], outs[n_row:], refs[2 * count :]
    )


def exchange(
    n_tok, n_mdl, rows_in, cols_in, rows_out, cols_out, semaphores, prepare=None, between=None
):
    n_row, n_col = len(rows_in), len(cols_in)
    (
        local_sem,
        send1,
        recv1,
        send2,
        recv2,
        send3,
        recv3,
        to_right,
        from_left,
        to_left,
        from_right,
    ) = semaphores
    square = n_tok == 8
    chips = n_tok // 2
    tok, mdl = lax.axis_index("tok"), lax.axis_index("mdl")
    chip, core = tok // 2, tok % 2
    sibling = chip * 2 + 1 - core

    def chip_at(step):
        if square:
            return (chip, chip + 1 - 2 * (chip % 2), (chip + 2) % 4, 3 - chip)[step]
        return (chip + step) % chips

    def source_at(step):
        return chip_at(step) if square else chip_at(chips - step)

    barrier = pltpu.get_barrier_semaphore()
    greeted = 0
    if n_row:
        for step in (1, 2) if square else range(1, chips):
            pl.semaphore_signal(
                barrier, inc=1, device_id={"tok": chip_at(step) * 2 + core, "mdl": mdl}
            )
            greeted += 1
        pl.semaphore_signal(barrier, inc=1, device_id={"tok": sibling, "mdl": mdl})
        greeted += 1
    if n_col:
        for side in (1, n_mdl - 1):
            pl.semaphore_signal(
                barrier, inc=1, device_id={"tok": tok, "mdl": (mdl + side) % n_mdl}
            )
            greeted += 1
    pl.semaphore_wait(barrier, greeted)

    def row_block(number, owner):
        size = rows_in[number].shape[0]
        return rows_out[number].at[pl.ds(pl.multiple_of(owner * size, size), size), :]

    def col_block(number, owner):
        size = cols_in[number].shape[1]
        return cols_out[number].at[:, pl.ds(pl.multiple_of(owner * size, size), size)]

    def direct(number, step):
        target = chip_at(step) * 2 + core if step else sibling
        return pltpu.make_async_remote_copy(
            src_ref=rows_in[number],
            dst_ref=row_block(number, tok),
            send_sem=send1.at[number, step],
            recv_sem=recv1.at[number, step],
            device_id={"tok": target, "mdl": mdl},
        )

    def passed(number, step):
        block = row_block(number, source_at(step) * 2 + core)
        return pltpu.make_async_remote_copy(
            src_ref=block,
            dst_ref=block,
            send_sem=send2.at[number, step],
            recv_sem=recv2.at[number, step],
            device_id={"tok": sibling, "mdl": mdl},
        )

    def relayed(number, step):
        half = rows_in[number].shape[0] // 2
        first = (source_at(step) * 2 + core) * 2 * half + (step - 1) * half
        block = rows_out[number].at[pl.ds(pl.multiple_of(first, half), half), :]
        return pltpu.make_async_remote_copy(
            src_ref=block,
            dst_ref=block,
            send_sem=send3.at[number, step],
            recv_sem=recv3.at[number, step],
            device_id={"tok": chip_at(3 - step) * 2 + core, "mdl": mdl},
        )

    directs = (1, 2) if square else range(1, chips)

    def rightward(number, step):
        block = col_block(number, mdl - step)
        return pltpu.make_async_remote_copy(
            src_ref=block if step else cols_in[number],
            dst_ref=block,
            send_sem=to_right.at[number, step],
            recv_sem=from_left.at[number, step],
            device_id={"tok": tok, "mdl": mdl + 1},
        )

    def leftward(number, step):
        block = col_block(number, mdl + step)
        return pltpu.make_async_remote_copy(
            src_ref=block if step else cols_in[number],
            dst_ref=block,
            send_sem=to_left.at[number, step],
            recv_sem=from_right.at[number, step],
            device_id={"tok": tok, "mdl": mdl - 1},
        )

    def right_if(step):
        return (mdl >= step) & (mdl < n_mdl - 1)

    def left_if(step):
        return (mdl + step < n_mdl) & (mdl > 0)

    for number in range(n_col):
        @pl.when(right_if(0))
        def _():
            rightward(number, 0).start()

        @pl.when(left_if(0))
        def _():
            leftward(number, 0).start()

    locals_ = []
    for number in range(n_col):
        locals_.append(
            pltpu.make_async_copy(
                cols_in[number], col_block(number, mdl), local_sem.at[n_row + number]
            )
        )
        locals_[-1].start()
    for number in range(n_row):
        if prepare is not None:
            prepare(number)
        for step in directs:
            direct(number, step).start()
        direct(number, 0).start()
        locals_.append(
            pltpu.make_async_copy(rows_in[number], row_block(number, tok), local_sem.at[number])
        )
        locals_[-1].start()

    def finish_diagonal(number):
        for step in (1, 2):
            relayed(number, step).wait_recv()
        passed(number, 3).start()

    for turn in range(max(n_row, n_mdl - 2 if n_col else 0)):
        hop = turn + 1
        if hop < n_mdl - 1:
            for number in range(n_col):
                @pl.when(mdl >= hop)
                def _():
                    rightward(number, hop - 1).wait_recv()

                @pl.when(right_if(hop))
                def _():
                    rightward(number, hop).start()

                @pl.when(mdl + hop < n_mdl)
                def _():
                    leftward(number, hop - 1).wait_recv()

                @pl.when(left_if(hop))
                def _():
                    leftward(number, hop).start()

        if turn < n_row:
            for step in directs:
                direct(turn, step).wait_recv()
                if square:
                    relayed(turn, step).start()
                passed(turn, step).start()
            if square and turn > 0:
                finish_diagonal(turn - 1)
        if between is not None:
            between(turn)

    if square and n_row:
        finish_diagonal(n_row - 1)
    for copy in locals_:
        copy.wait()
    for number in range(n_col):
        @pl.when(mdl >= n_mdl - 1)
        def _():
            rightward(number, n_mdl - 2).wait_recv()

        @pl.when(mdl + n_mdl - 1 < n_mdl)
        def _():
            leftward(number, n_mdl - 2).wait_recv()

    for number in range(n_row):
        direct(number, 0).wait()
        for step in directs:
            direct(number, step).wait_send()
            if square:
                relayed(number, step).wait_send()
        for step in range(1, chips):
            passed(number, step).wait()
    for number in range(n_col):
        for step in range(n_mdl - 1):
            @pl.when(right_if(step))
            def _():
                rightward(number, step).wait_send()

            @pl.when(left_if(step))
            def _():
                leftward(number, step).wait_send()


def exchange_semaphores(n_tok, n_mdl, n_row, n_col):
    row_sem = pltpu.SemaphoreType.DMA((max(n_row, 1), n_tok // 2))
    col_sem = pltpu.SemaphoreType.DMA((max(n_col, 1), n_mdl))
    return [pltpu.SemaphoreType.DMA((n_row + n_col,))] + [row_sem] * 6 + [col_sem] * 4


def project_kernel(n_tok, n_mdl, head_width, *refs):
    normed, key_w, value_w, query_w, key_gain, query_gain, cosine, sine = refs[:8]
    keys_out, values_out, query_out = refs[8:11]
    keys, values, query, key_held, value_held, query_held, load_sem = refs[11:18]
    width = keys.shape[1]
    lanes = 2 * head_width
    block = 256 if width % 256 == 0 else lanes
    loads = [
        pltpu.make_async_copy(source, held, load_sem.at[number])
        for number, (source, held) in enumerate(
            ((key_w, key_held), (value_w, value_held), (query_w, query_held))
        )
    ]
    for load in loads:
        load.start()
    lane = lax.broadcasted_iota(jnp.int32, (1, lanes), 1)
    first = lane < head_width
    early = lane % head_width < head_width // 2

    def head_mean(terms):
        one = jnp.sum(jnp.where(first, terms, 0.0), axis=1, keepdims=True)
        other = jnp.sum(jnp.where(first, 0.0, terms), axis=1, keepdims=True)
        return jnp.where(first, one, other) * (1.0 / head_width)

    def finished(summed, gain):
        center = summed - head_mean(summed)
        normal = center * lax.rsqrt(head_mean(center * center) + 1e-06) * gain[...]
        partner = jnp.where(
            early,
            pltpu.roll(normal, lanes - head_width // 2, axis=1),
            pltpu.roll(normal, head_width // 2, axis=1),
        )
        return normal * cosine[...] + partner * sine[...]

    def project(held, gain, target):
        def step(number, carry):
            columns = pl.ds(pl.multiple_of(number * block, block), block)
            summed = jnp.dot(
                normed[...], held[:, columns], preferred_element_type=jnp.float32
            )
            if gain is not None:
                summed = jnp.concatenate(
                    [
                        finished(summed[:, start : start + lanes], gain)
                        for start in range(0, block, lanes)
                    ],
                    axis=1,
                )
            target[:, columns] = summed.astype(jnp.bfloat16)
            return carry

        lax.fori_loop(0, width // block, step, 0)

    def prepare(number):
        loads[number].wait()
        if number == 0:
            project(key_held, key_gain, keys)
        else:
            project(value_held, None, values)

    query_copy = pltpu.make_async_copy(query, query_out, load_sem.at[3])

    def between(turn):
        if turn == 0:
            loads[2].wait()
            project(query_held, query_gain, query)
            query_copy.start()

    exchange(
        n_tok,
        n_mdl,
        (keys, values),
        (),
        (keys_out, values_out),
        (),
        refs[18:],
        prepare,
        between,
    )
    query_copy.wait()


def project_and_gather(mesh, normed, weights, gains, cosine, sine, head_width, collective_id):
    n_tok, n_mdl = mesh.shape["tok"], mesh.shape["mdl"]
    own_rows, depth = normed.shape
    width = weights[0].shape[1]
    full = jax.ShapeDtypeStruct((own_rows * n_tok, width), jnp.bfloat16)
    own = jax.ShapeDtypeStruct((own_rows, width), jnp.bfloat16)
    anywhere = pl.BlockSpec(memory_space=pl.ANY)
    inside = pl.BlockSpec(memory_space=pltpu.VMEM)
    return pl.pallas_call(
        functools.partial(project_kernel, n_tok, n_mdl, head_width),
        out_shape=[full, full, own],
        in_specs=[inside] + [anywhere] * 3 + [inside] * 4,
        out_specs=[anywhere] * 3,
        scratch_shapes=[pltpu.VMEM((own_rows, width), jnp.bfloat16)] * 3
        + [pltpu.VMEM((depth, width), jnp.bfloat16)] * 3
        + [pltpu.SemaphoreType.DMA((4,))]
        + exchange_semaphores(n_tok, n_mdl, 2, 0),
        compiler_params=pltpu.CompilerParams(
            collective_id=collective_id, has_side_effects=True, vmem_limit_bytes=48 * 2**20
        ),
        name="project_and_gather",
    )(normed, *weights, *gains, cosine, sine)


def gather_all(mesh, over_tok, over_mdl, collective_id):
    n_tok, n_mdl = mesh.shape["tok"], mesh.shape["mdl"]
    n_row, n_col = len(over_tok), len(over_mdl)
    shapes = [
        jax.ShapeDtypeStruct((one.shape[0] * n_tok, one.shape[1]), one.dtype) for one in over_tok
    ] + [jax.ShapeDtypeStruct((one.shape[0], one.shape[1] * n_mdl), one.dtype) for one in over_mdl]
    return pl.pallas_call(
        functools.partial(gather_kernel, n_tok, n_mdl, n_row, n_col),
        out_shape=shapes,
        in_specs=[pl.BlockSpec(memory_space=pl.ANY)] * (n_row + n_col),
        out_specs=[pl.BlockSpec(memory_space=pl.ANY)] * (n_row + n_col),
        scratch_shapes=exchange_semaphores(n_tok, n_mdl, n_row, n_col),
        compiler_params=pltpu.CompilerParams(collective_id=collective_id, has_side_effects=True),
        name=f"gather_{collective_id}",
    )(*over_tok, *over_mdl)


def attend_kernel(rows_at_once, keys_at_once, head_width, meta_ref, q_ref, k_ref, v_ref, o_ref):
    bound, first_row = meta_ref[0], meta_ref[1]
    own_rows, lanes = q_ref.shape
    count = k_ref.shape[0]
    chunks = count // keys_at_once
    per = lanes // head_width
    lane = lax.broadcasted_iota(jnp.int32, (1, lanes), 1) // head_width
    masks = [(lane == head).astype(jnp.float32) for head in range(per)]
    edge = bound // keys_at_once
    edge_start = pl.multiple_of(edge * keys_at_once, keys_at_once)
    edge_keys = edge_start + lax.broadcasted_iota(jnp.int32, (keys_at_once, 1), 0)

    for block in range(own_rows // rows_at_once):
        rows = pl.ds(block * rows_at_once, rows_at_once)
        start = first_row + block * rows_at_once
        row_ids = start + lax.broadcasted_iota(jnp.int32, (rows_at_once, 1), 0)

        def add_chunk(carry, keys, values):
            queries = q_ref[rows, :]
            result = []
            for head in range(per):
                mine = queries * (masks[head] * head_width ** (-0.5)).astype(jnp.bfloat16)
                score = lax.dot_general(
                    mine, keys, (((1,), (1,)), ((), ())), preferred_element_type=jnp.float32
                )
                expo = jnp.exp(score).astype(jnp.bfloat16)
                result.append(
                    carry[head]
                    + jnp.dot(expo, values[head], preferred_element_type=jnp.float32)
                )
            return tuple(result)

        def inner(chunk, carry):
            here = pl.ds(pl.multiple_of(chunk * keys_at_once, keys_at_once), keys_at_once)
            values = v_ref[here, :]
            with_ones = [
                values * mask.astype(jnp.bfloat16) + (1.0 - mask).astype(jnp.bfloat16)
                for mask in masks
            ]
            return add_chunk(carry, k_ref[here, :], with_ones)

        for request in range(2):
            active = start < bound if request == 0 else start + rows_at_once > bound

            @pl.when(active)
            def _():
                here = pl.ds(edge_start, keys_at_once)
                inside = edge_keys < bound if request == 0 else edge_keys >= bound
                wide = v_ref[here, :].astype(jnp.float32)
                with_ones = [
                    jnp.where(inside, wide * mask + (1.0 - mask), 0.0).astype(jnp.bfloat16)
                    for mask in masks
                ]
                zero = jnp.zeros((rows_at_once, lanes), jnp.float32)
                carry = add_chunk((zero,) * per, k_ref[here, :], with_ones)
                if request == 0:
                    low, high = 0, edge
                else:
                    low, high = edge + 1, chunks
                carry = lax.fori_loop(low, high, inner, carry)
                output = zero
                for head in range(per):
                    total = pltpu.roll(carry[head], head_width, axis=1)
                    output = jnp.where(lane == head, carry[head] / total, output)
                if request == 0:
                    o_ref[rows, :] = output.astype(o_ref.dtype)
                else:
                    old = o_ref[rows, :].astype(jnp.float32)
                    o_ref[rows, :] = jnp.where(row_ids >= bound, output, old).astype(o_ref.dtype)


def attend(query, keys, values, bound, first_row, head_width, part, parts):
    width = query.shape[1]
    own_rows = query.shape[0] // parts
    count = keys.shape[0]
    lanes = 2 * head_width
    meta = jnp.stack([bound, first_row + part * own_rows]).astype(jnp.int32)
    block = pl.BlockSpec((own_rows, lanes), lambda pair, meta: (part, pair))
    out_block = pl.BlockSpec((own_rows, lanes), lambda pair, meta: (0, pair))
    full = pl.BlockSpec((count, lanes), lambda pair, meta: (0, pair))
    return pl.pallas_call(
        functools.partial(attend_kernel, 256, 512, head_width),
        out_shape=jax.ShapeDtypeStruct((own_rows, width), jnp.bfloat16),
        grid_spec=pltpu.PrefetchScalarGridSpec(
            num_scalar_prefetch=1,
            grid=(width // lanes,),
            in_specs=[block, full, full],
            out_specs=out_block,
        ),
        compiler_params=pltpu.CompilerParams(vmem_limit_bytes=58 * 2**20),
        cost_estimate=pl.CostEstimate(
            flops=4 * own_rows * count * width,
            bytes_accessed=4 * count * width,
            transcendentals=own_rows * count * width // head_width,
        ),
        name=f"attend_{part}",
    )(meta, query, keys, values)


def shards(
    mesh,
    hidden_states,
    lengths,
    positions,
    modulation,
    query_weight,
    key_weight,
    value_weight,
    out_weight,
    query_gain,
    key_gain,
):
    own_rows = hidden_states.shape[0]
    head_width = query_gain.shape[0]
    key_full, value_full, query_full, full_rows = gather_all(
        mesh, [key_weight, value_weight, query_weight], [hidden_states], 0
    )
    row_index = lax.axis_index("tok") * own_rows + jnp.arange(own_rows, dtype=jnp.int32)
    request, is_text, bound = token_labels(row_index, lengths)
    normed = modulate(full_rows, modulation, is_text)
    angles = pair_angles(positions, head_width // 2)
    textual = is_text[:, None]
    cosine = jnp.tile(jnp.where(textual, 1.0, jnp.cos(angles)), (1, 4))
    sine = jnp.where(textual, 0.0, jnp.sin(angles))
    sine = jnp.tile(jnp.concatenate([-sine, sine], axis=1), (1, 2))
    keys, values, query_flat = project_and_gather(
        mesh,
        normed,
        (key_full, value_full, query_full),
        [jnp.tile(gain, 2)[None, :] for gain in (key_gain, query_gain)],
        cosine,
        sine,
        head_width,
        1,
    )
    first_row = lax.axis_index("tok") * own_rows
    first, second = (
        attend(query_flat, keys, values, bound, first_row, head_width, part, 2)
        for part in range(2)
    )
    first_heads = lax.all_gather(first, "mdl", axis=1, tiled=True)
    out_full, second_heads = gather_all(mesh, [out_weight], [second], 2)
    out_width = out_weight.shape[1]
    projected = jnp.concatenate(
        [
            jnp.dot(heads, out_full, preferred_element_type=jnp.float32)
            for heads in (first_heads, second_heads)
        ],
        axis=0,
    )
    gate_rows = lax.dynamic_slice_in_dim(
        modulation, lax.axis_index("mdl") * out_width, out_width, 1
    )
    gate = jnp.where(is_text[:, None], gate_rows[5][None, :], gate_rows[2][None, :])
    return (hidden_states.astype(jnp.float32) + gate * projected).astype(jnp.bfloat16)


def solution(mesh):
    return jax.shard_map(
        functools.partial(shards, mesh),
        mesh=mesh,
        in_specs=(
            P("tok", "mdl"),
            P(),
            P(None, "tok"),
            P(),
            P("tok", "mdl"),
            P("tok", "mdl"),
            P("tok", "mdl"),
            P("tok", "mdl"),
            P(),
            P(),
        ),
        out_specs=P("tok", "mdl"),
        check_vma=False,
    )
```

```python
import functools
import jax
import jax.numpy as jnp
from jax import lax
from jax.experimental import pallas as pl
from jax.experimental.pallas import tpu as pltpu
from jax.sharding import PartitionSpec as P

TEXT = 226


def token_labels(row_index, lengths):
    bound = TEXT + lengths[0]
    request = (row_index >= bound).astype(jnp.int32)
    place = row_index - request * bound
    return (request, place < TEXT, bound)


def modulate(rows_bf, modulation, is_text):
    values = rows_bf.astype(jnp.float32)
    center = values - jnp.mean(values, axis=1, keepdims=True)
    spread = jnp.mean(center * center, axis=1, keepdims=True)
    normal = center * lax.rsqrt(spread + 1e-05)
    textual = is_text[:, None]
    shift = jnp.where(textual, modulation[3][None, :], modulation[0][None, :])
    scale = jnp.where(textual, modulation[4][None, :], modulation[1][None, :])
    return (normal * (1.0 + scale) + shift).astype(jnp.bfloat16)


def pair_angles(positions, pairs):
    index = jnp.arange(pairs, dtype=jnp.int32)
    first = pairs // 4
    second = (pairs - first) // 2
    third = pairs - first - second
    component = jnp.where(index < first, 0, jnp.where(index < first + second, 1, 2))
    local = index - jnp.where(component == 0, 0, jnp.where(component == 1, first, first + second))
    count = jnp.where(component == 0, first, jnp.where(component == 1, second, third))
    rates = jnp.power(jnp.float32(10000.0), -local.astype(jnp.float32) / count.astype(jnp.float32))
    places = positions.astype(jnp.float32)
    chosen = jnp.where(
        component[:, None] == 0,
        places[0][None, :],
        jnp.where(component[:, None] == 1, places[1][None, :], places[2][None, :]),
    )
    return jnp.transpose(chosen * rates[:, None])


def gather_kernel(n_tok, n_mdl, n_row, n_col, *refs):
    count = n_row + n_col
    ins, outs = refs[:count], refs[count : 2 * count]
    exchange(
        n_tok, n_mdl, ins[:n_row], ins[n_row:], outs[:n_row], outs[n_row:], refs[2 * count :]
    )


def exchange(
    n_tok, n_mdl, rows_in, cols_in, rows_out, cols_out, semaphores, prepare=None, between=None
):
    n_row, n_col = len(rows_in), len(cols_in)
    (
        local_sem,
        send1,
        recv1,
        send2,
        recv2,
        send3,
        recv3,
        to_right,
        from_left,
        to_left,
        from_right,
    ) = semaphores
    square = n_tok == 8
    chips = n_tok // 2
    tok, mdl = lax.axis_index("tok"), lax.axis_index("mdl")
    chip, core = tok // 2, tok % 2
    sibling = chip * 2 + 1 - core

    def chip_at(step):
        if square:
            return (chip, chip + 1 - 2 * (chip % 2), (chip + 2) % 4, 3 - chip)[step]
        return (chip + step) % chips

    def source_at(step):
        return chip_at(step) if square else chip_at(chips - step)

    barrier = pltpu.get_barrier_semaphore()
    greeted = 0
    if n_row:
        for step in (1, 2) if square else range(1, chips):
            pl.semaphore_signal(
                barrier, inc=1, device_id={"tok": chip_at(step) * 2 + core, "mdl": mdl}
            )
            greeted += 1
        pl.semaphore_signal(barrier, inc=1, device_id={"tok": sibling, "mdl": mdl})
        greeted += 1
    if n_col:
        for side in (1, n_mdl - 1):
            pl.semaphore_signal(
                barrier, inc=1, device_id={"tok": tok, "mdl": (mdl + side) % n_mdl}
            )
            greeted += 1
    pl.semaphore_wait(barrier, greeted)

    def row_block(number, owner):
        size = rows_in[number].shape[0]
        return rows_out[number].at[pl.ds(pl.multiple_of(owner * size, size), size), :]

    def col_block(number, owner):
        size = cols_in[number].shape[1]
        return cols_out[number].at[:, pl.ds(pl.multiple_of(owner * size, size), size)]

    def direct(number, step):
        target = chip_at(step) * 2 + core if step else sibling
        return pltpu.make_async_remote_copy(
            src_ref=rows_in[number],
            dst_ref=row_block(number, tok),
            send_sem=send1.at[number, step],
            recv_sem=recv1.at[number, step],
            device_id={"tok": target, "mdl": mdl},
        )

    def passed(number, step):
        block = row_block(number, source_at(step) * 2 + core)
        return pltpu.make_async_remote_copy(
            src_ref=block,
            dst_ref=block,
            send_sem=send2.at[number, step],
            recv_sem=recv2.at[number, step],
            device_id={"tok": sibling, "mdl": mdl},
        )

    def relayed(number, step):
        half = rows_in[number].shape[0] // 2
        first = (source_at(step) * 2 + core) * 2 * half + (step - 1) * half
        block = rows_out[number].at[pl.ds(pl.multiple_of(first, half), half), :]
        return pltpu.make_async_remote_copy(
            src_ref=block,
            dst_ref=block,
            send_sem=send3.at[number, step],
            recv_sem=recv3.at[number, step],
            device_id={"tok": chip_at(3 - step) * 2 + core, "mdl": mdl},
        )

    directs = (1, 2) if square else range(1, chips)

    def rightward(number, step):
        block = col_block(number, mdl - step)
        return pltpu.make_async_remote_copy(
            src_ref=block if step else cols_in[number],
            dst_ref=block,
            send_sem=to_right.at[number, step],
            recv_sem=from_left.at[number, step],
            device_id={"tok": tok, "mdl": mdl + 1},
        )

    def leftward(number, step):
        block = col_block(number, mdl + step)
        return pltpu.make_async_remote_copy(
            src_ref=block if step else cols_in[number],
            dst_ref=block,
            send_sem=to_left.at[number, step],
            recv_sem=from_right.at[number, step],
            device_id={"tok": tok, "mdl": mdl - 1},
        )

    def right_if(step):
        return (mdl >= step) & (mdl < n_mdl - 1)

    def left_if(step):
        return (mdl + step < n_mdl) & (mdl > 0)

    for number in range(n_col):
        @pl.when(right_if(0))
        def _():
            rightward(number, 0).start()

        @pl.when(left_if(0))
        def _():
            leftward(number, 0).start()

    locals_ = []
    for number in range(n_col):
        locals_.append(
            pltpu.make_async_copy(
                cols_in[number], col_block(number, mdl), local_sem.at[n_row + number]
            )
        )
        locals_[-1].start()
    for number in range(n_row):
        if prepare is not None:
            prepare(number)
        for step in directs:
            direct(number, step).start()
        direct(number, 0).start()
        locals_.append(
            pltpu.make_async_copy(rows_in[number], row_block(number, tok), local_sem.at[number])
        )
        locals_[-1].start()

    def finish_diagonal(number):
        for step in (1, 2):
            relayed(number, step).wait_recv()
        passed(number, 3).start()

    for turn in range(max(n_row, n_mdl - 2 if n_col else 0)):
        hop = turn + 1
        if hop < n_mdl - 1:
            for number in range(n_col):
                @pl.when(mdl >= hop)
                def _():
                    rightward(number, hop - 1).wait_recv()

                @pl.when(right_if(hop))
                def _():
                    rightward(number, hop).start()

                @pl.when(mdl + hop < n_mdl)
                def _():
                    leftward(number, hop - 1).wait_recv()

                @pl.when(left_if(hop))
                def _():
                    leftward(number, hop).start()

        if turn < n_row:
            for step in directs:
                direct(turn, step).wait_recv()
                if square:
                    relayed(turn, step).start()
                passed(turn, step).start()
            if square and turn > 0:
                finish_diagonal(turn - 1)
        if between is not None:
            between(turn)

    if square and n_row:
        finish_diagonal(n_row - 1)
    for copy in locals_:
        copy.wait()
    for number in range(n_col):
        @pl.when(mdl >= n_mdl - 1)
        def _():
            rightward(number, n_mdl - 2).wait_recv()

        @pl.when(mdl + n_mdl - 1 < n_mdl)
        def _():
            leftward(number, n_mdl - 2).wait_recv()

    for number in range(n_row):
        direct(number, 0).wait()
        for step in directs:
            direct(number, step).wait_send()
            if square:
                relayed(number, step).wait_send()
        for step in range(1, chips):
            passed(number, step).wait()
    for number in range(n_col):
        for step in range(n_mdl - 1):
            @pl.when(right_if(step))
            def _():
                rightward(number, step).wait_send()

            @pl.when(left_if(step))
            def _():
                leftward(number, step).wait_send()


def exchange_semaphores(n_tok, n_mdl, n_row, n_col):
    row_sem = pltpu.SemaphoreType.DMA((max(n_row, 1), n_tok // 2))
    col_sem = pltpu.SemaphoreType.DMA((max(n_col, 1), n_mdl))
    return [pltpu.SemaphoreType.DMA((n_row + n_col,))] + [row_sem] * 6 + [col_sem] * 4


def project_kernel(n_tok, n_mdl, head_width, *refs):
    normed, key_w, value_w, query_w, key_gain, query_gain, cosine, sine = refs[:8]
    keys_out, values_out, query_out = refs[8:11]
    keys, values, query, key_held, value_held, query_held, load_sem = refs[11:18]
    width = keys.shape[1]
    lanes = 2 * head_width
    block = 256 if width % 256 == 0 else lanes
    loads = [
        pltpu.make_async_copy(source, held, load_sem.at[number])
        for number, (source, held) in enumerate(
            ((key_w, key_held), (value_w, value_held), (query_w, query_held))
        )
    ]
    for load in loads:
        load.start()
    lane = lax.broadcasted_iota(jnp.int32, (1, lanes), 1)
    first = lane < head_width
    early = lane % head_width < head_width // 2

    def head_mean(terms):
        one = jnp.sum(jnp.where(first, terms, 0.0), axis=1, keepdims=True)
        other = jnp.sum(jnp.where(first, 0.0, terms), axis=1, keepdims=True)
        return jnp.where(first, one, other) * (1.0 / head_width)

    def finished(summed, gain):
        center = summed - head_mean(summed)
        normal = center * lax.rsqrt(head_mean(center * center) + 1e-06) * gain[...]
        partner = jnp.where(
            early,
            pltpu.roll(normal, lanes - head_width // 2, axis=1),
            pltpu.roll(normal, head_width // 2, axis=1),
        )
        return normal * cosine[...] + partner * sine[...]

    def project(held, gain, target):
        def step(number, carry):
            columns = pl.ds(pl.multiple_of(number * block, block), block)
            summed = jnp.dot(
                normed[...], held[:, columns], preferred_element_type=jnp.float32
            )
            if gain is not None:
                summed = jnp.concatenate(
                    [
                        finished(summed[:, start : start + lanes], gain)
                        for start in range(0, block, lanes)
                    ],
                    axis=1,
                )
            target[:, columns] = summed.astype(jnp.bfloat16)
            return carry

        lax.fori_loop(0, width // block, step, 0)

    def prepare(number):
        loads[number].wait()
        if number == 0:
            project(key_held, key_gain, keys)
        else:
            project(value_held, None, values)

    query_copy = pltpu.make_async_copy(query, query_out, load_sem.at[3])

    def between(turn):
        if turn == 0:
            loads[2].wait()
            project(query_held, query_gain, query)
            query_copy.start()

    exchange(
        n_tok,
        n_mdl,
        (keys, values),
        (),
        (keys_out, values_out),
        (),
        refs[18:],
        prepare,
        between,
    )
    query_copy.wait()


def project_and_gather(mesh, normed, weights, gains, cosine, sine, head_width, collective_id):
    n_tok, n_mdl = mesh.shape["tok"], mesh.shape["mdl"]
    own_rows, depth = normed.shape
    width = weights[0].shape[1]
    full = jax.ShapeDtypeStruct((own_rows * n_tok, width), jnp.bfloat16)
    own = jax.ShapeDtypeStruct((own_rows, width), jnp.bfloat16)
    anywhere = pl.BlockSpec(memory_space=pl.ANY)
    inside = pl.BlockSpec(memory_space=pltpu.VMEM)
    return pl.pallas_call(
        functools.partial(project_kernel, n_tok, n_mdl, head_width),
        out_shape=[full, full, own],
        in_specs=[inside] + [anywhere] * 3 + [inside] * 4,
        out_specs=[anywhere] * 3,
        scratch_shapes=[pltpu.VMEM((own_rows, width), jnp.bfloat16)] * 3
        + [pltpu.VMEM((depth, width), jnp.bfloat16)] * 3
        + [pltpu.SemaphoreType.DMA((4,))]
        + exchange_semaphores(n_tok, n_mdl, 2, 0),
        compiler_params=pltpu.CompilerParams(
            collective_id=collective_id, has_side_effects=True, vmem_limit_bytes=48 * 2**20
        ),
        name="project_and_gather",
    )(normed, *weights, *gains, cosine, sine)


def gather_all(mesh, over_tok, over_mdl, collective_id):
    n_tok, n_mdl = mesh.shape["tok"], mesh.shape["mdl"]
    n_row, n_col = len(over_tok), len(over_mdl)
    shapes = [
        jax.ShapeDtypeStruct((one.shape[0] * n_tok, one.shape[1]), one.dtype) for one in over_tok
    ] + [jax.ShapeDtypeStruct((one.shape[0], one.shape[1] * n_mdl), one.dtype) for one in over_mdl]
    return pl.pallas_call(
        functools.partial(gather_kernel, n_tok, n_mdl, n_row, n_col),
        out_shape=shapes,
        in_specs=[pl.BlockSpec(memory_space=pl.ANY)] * (n_row + n_col),
        out_specs=[pl.BlockSpec(memory_space=pl.ANY)] * (n_row + n_col),
        scratch_shapes=exchange_semaphores(n_tok, n_mdl, n_row, n_col),
        compiler_params=pltpu.CompilerParams(collective_id=collective_id, has_side_effects=True),
        name=f"gather_{collective_id}",
    )(*over_tok, *over_mdl)


def attend_kernel(rows_at_once, keys_at_once, head_width, meta_ref, q_ref, k_ref, v_ref, o_ref):
    bound, first_row = meta_ref[0], meta_ref[1]
    own_rows, lanes = q_ref.shape
    count = k_ref.shape[0]
    chunks = count // keys_at_once
    per = lanes // head_width
    lane = lax.broadcasted_iota(jnp.int32, (1, lanes), 1) // head_width
    masks = [(lane == head).astype(jnp.float32) for head in range(per)]
    edge = bound // keys_at_once
    edge_start = pl.multiple_of(edge * keys_at_once, keys_at_once)
    edge_keys = edge_start + lax.broadcasted_iota(jnp.int32, (keys_at_once, 1), 0)

    for block in range(own_rows // rows_at_once):
        rows = pl.ds(block * rows_at_once, rows_at_once)
        start = first_row + block * rows_at_once
        row_ids = start + lax.broadcasted_iota(jnp.int32, (rows_at_once, 1), 0)

        def add_chunk(carry, keys, values):
            queries = q_ref[rows, :]
            result = []
            for head in range(per):
                mine = queries * (masks[head] * head_width ** (-0.5)).astype(jnp.bfloat16)
                score = lax.dot_general(
                    mine, keys, (((1,), (1,)), ((), ())), preferred_element_type=jnp.float32
                )
                expo = jnp.exp(score).astype(jnp.bfloat16)
                result.append(
                    carry[head]
                    + jnp.dot(expo, values[head], preferred_element_type=jnp.float32)
                )
            return tuple(result)

        def inner(chunk, carry):
            here = pl.ds(pl.multiple_of(chunk * keys_at_once, keys_at_once), keys_at_once)
            values = v_ref[here, :]
            with_ones = [
                values * mask.astype(jnp.bfloat16) + (1.0 - mask).astype(jnp.bfloat16)
                for mask in masks
            ]
            return add_chunk(carry, k_ref[here, :], with_ones)

        for request in range(2):
            active = start < bound if request == 0 else start + rows_at_once > bound

            @pl.when(active)
            def _():
                here = pl.ds(edge_start, keys_at_once)
                inside = edge_keys < bound if request == 0 else edge_keys >= bound
                wide = v_ref[here, :].astype(jnp.float32)
                with_ones = [
                    jnp.where(inside, wide * mask + (1.0 - mask), 0.0).astype(jnp.bfloat16)
                    for mask in masks
                ]
                zero = jnp.zeros((rows_at_once, lanes), jnp.float32)
                carry = add_chunk((zero,) * per, k_ref[here, :], with_ones)
                if request == 0:
                    low, high = 0, edge
                else:
                    low, high = edge + 1, chunks
                carry = lax.fori_loop(low, high, inner, carry)
                output = zero
                for head in range(per):
                    total = pltpu.roll(carry[head], head_width, axis=1)
                    output = jnp.where(lane == head, carry[head] / total, output)
                if request == 0:
                    o_ref[rows, :] = output.astype(o_ref.dtype)
                else:
                    old = o_ref[rows, :].astype(jnp.float32)
                    o_ref[rows, :] = jnp.where(row_ids >= bound, output, old).astype(o_ref.dtype)


def attend(query, keys, values, bound, first_row, head_width, part, parts):
    width = query.shape[1]
    own_rows = query.shape[0] // parts
    count = keys.shape[0]
    lanes = 2 * head_width
    meta = jnp.stack([bound, first_row + part * own_rows]).astype(jnp.int32)
    block = pl.BlockSpec((own_rows, lanes), lambda pair, meta: (part, pair))
    out_block = pl.BlockSpec((own_rows, lanes), lambda pair, meta: (0, pair))
    full = pl.BlockSpec((count, lanes), lambda pair, meta: (0, pair))
    return pl.pallas_call(
        functools.partial(attend_kernel, 256, 512, head_width),
        out_shape=jax.ShapeDtypeStruct((own_rows, width), jnp.bfloat16),
        grid_spec=pltpu.PrefetchScalarGridSpec(
            num_scalar_prefetch=1,
            grid=(width // lanes,),
            in_specs=[block, full, full],
            out_specs=out_block,
        ),
        compiler_params=pltpu.CompilerParams(vmem_limit_bytes=58 * 2**20),
        cost_estimate=pl.CostEstimate(
            flops=4 * own_rows * count * width,
            bytes_accessed=4 * count * width,
            transcendentals=own_rows * count * width // head_width,
        ),
        name=f"attend_{part}",
    )(meta, query, keys, values)


def shards(
    mesh,
    hidden_states,
    lengths,
    positions,
    modulation,
    query_weight,
    key_weight,
    value_weight,
    out_weight,
    query_gain,
    key_gain,
):
    own_rows = hidden_states.shape[0]
    head_width = query_gain.shape[0]
    full_rows = lax.all_gather(hidden_states, "mdl", axis=1, tiled=True)
    key_full, value_full, query_full = gather_all(
        mesh, [key_weight, value_weight, query_weight], [], 0
    )
    row_index = lax.axis_index("tok") * own_rows + jnp.arange(own_rows, dtype=jnp.int32)
    request, is_text, bound = token_labels(row_index, lengths)
    normed = modulate(full_rows, modulation, is_text)
    angles = pair_angles(positions, head_width // 2)
    textual = is_text[:, None]
    cosine = jnp.tile(jnp.where(textual, 1.0, jnp.cos(angles)), (1, 4))
    sine = jnp.where(textual, 0.0, jnp.sin(angles))
    sine = jnp.tile(jnp.concatenate([-sine, sine], axis=1), (1, 2))
    keys, values, query_flat = project_and_gather(
        mesh,
        normed,
        (key_full, value_full, query_full),
        [jnp.tile(gain, 2)[None, :] for gain in (key_gain, query_gain)],
        cosine,
        sine,
        head_width,
        1,
    )
    first_row = lax.axis_index("tok") * own_rows
    first, second = (
        attend(query_flat, keys, values, bound, first_row, head_width, part, 2)
        for part in range(2)
    )
    first_heads = lax.all_gather(first, "mdl", axis=1, tiled=True)
    out_full, second_heads = gather_all(mesh, [out_weight], [second], 2)
    out_width = out_weight.shape[1]
    projected = jnp.concatenate(
        [
            jnp.dot(heads, out_full, preferred_element_type=jnp.float32)
            for heads in (first_heads, second_heads)
        ],
        axis=0,
    )
    gate_rows = lax.dynamic_slice_in_dim(
        modulation, lax.axis_index("mdl") * out_width, out_width, 1
    )
    gate = jnp.where(is_text[:, None], gate_rows[5][None, :], gate_rows[2][None, :])
    return (hidden_states.astype(jnp.float32) + gate * projected).astype(jnp.bfloat16)


def solution(mesh):
    return jax.shard_map(
        functools.partial(shards, mesh),
        mesh=mesh,
        in_specs=(
            P("tok", "mdl"),
            P(),
            P(None, "tok"),
            P(),
            P("tok", "mdl"),
            P("tok", "mdl"),
            P("tok", "mdl"),
            P("tok", "mdl"),
            P(),
            P(),
        ),
        out_specs=P("tok", "mdl"),
        check_vma=False,
    )
```

```python
import functools
import jax
import jax.numpy as jnp
from jax import lax
from jax.experimental import pallas as pl
from jax.experimental.pallas import tpu as pltpu
from jax.sharding import PartitionSpec as P

TEXT = 226


def token_labels(row_index, lengths):
    bound = TEXT + lengths[0]
    request = (row_index >= bound).astype(jnp.int32)
    place = row_index - request * bound
    return (request, place < TEXT, bound)


def modulate(rows_bf, modulation, is_text):
    values = rows_bf.astype(jnp.float32)
    center = values - jnp.mean(values, axis=1, keepdims=True)
    spread = jnp.mean(center * center, axis=1, keepdims=True)
    normal = center * lax.rsqrt(spread + 1e-05)
    textual = is_text[:, None]
    shift = jnp.where(textual, modulation[3][None, :], modulation[0][None, :])
    scale = jnp.where(textual, modulation[4][None, :], modulation[1][None, :])
    return (normal * (1.0 + scale) + shift).astype(jnp.bfloat16)


def pair_angles(positions, pairs):
    index = jnp.arange(pairs, dtype=jnp.int32)
    first = pairs // 4
    second = (pairs - first) // 2
    third = pairs - first - second
    component = jnp.where(index < first, 0, jnp.where(index < first + second, 1, 2))
    local = index - jnp.where(component == 0, 0, jnp.where(component == 1, first, first + second))
    count = jnp.where(component == 0, first, jnp.where(component == 1, second, third))
    rates = jnp.power(jnp.float32(10000.0), -local.astype(jnp.float32) / count.astype(jnp.float32))
    places = positions.astype(jnp.float32)
    chosen = jnp.where(
        component[:, None] == 0,
        places[0][None, :],
        jnp.where(component[:, None] == 1, places[1][None, :], places[2][None, :]),
    )
    return jnp.transpose(chosen * rates[:, None])


def gather_kernel(n_tok, n_mdl, n_row, n_col, *refs):
    count = n_row + n_col
    ins, outs = refs[:count], refs[count : 2 * count]
    exchange(
        n_tok, n_mdl, ins[:n_row], ins[n_row:], outs[:n_row], outs[n_row:], refs[2 * count :]
    )


def exchange(
    n_tok, n_mdl, rows_in, cols_in, rows_out, cols_out, semaphores, prepare=None, between=None
):
    n_row, n_col = len(rows_in), len(cols_in)
    (
        local_sem,
        send1,
        recv1,
        send2,
        recv2,
        send3,
        recv3,
        to_right,
        from_left,
        to_left,
        from_right,
    ) = semaphores
    square = n_tok == 8
    chips = n_tok // 2
    tok, mdl = lax.axis_index("tok"), lax.axis_index("mdl")
    chip, core = tok // 2, tok % 2
    sibling = chip * 2 + 1 - core

    def chip_at(step):
        if square:
            return (chip, chip + 1 - 2 * (chip % 2), (chip + 2) % 4, 3 - chip)[step]
        return (chip + step) % chips

    def source_at(step):
        return chip_at(step) if square else chip_at(chips - step)

    barrier = pltpu.get_barrier_semaphore()
    greeted = 0
    if n_row:
        for step in (1, 2) if square else range(1, chips):
            pl.semaphore_signal(
                barrier, inc=1, device_id={"tok": chip_at(step) * 2 + core, "mdl": mdl}
            )
            greeted += 1
        pl.semaphore_signal(barrier, inc=1, device_id={"tok": sibling, "mdl": mdl})
        greeted += 1
    if n_col:
        for side in (1, n_mdl - 1):
            pl.semaphore_signal(
                barrier, inc=1, device_id={"tok": tok, "mdl": (mdl + side) % n_mdl}
            )
            greeted += 1
    pl.semaphore_wait(barrier, greeted)

    def row_block(number, owner):
        size = rows_in[number].shape[0]
        return rows_out[number].at[pl.ds(pl.multiple_of(owner * size, size), size), :]

    def col_block(number, owner):
        size = cols_in[number].shape[1]
        return cols_out[number].at[:, pl.ds(pl.multiple_of(owner * size, size), size)]

    def direct(number, step):
        target = chip_at(step) * 2 + core if step else sibling
        return pltpu.make_async_remote_copy(
            src_ref=rows_in[number],
            dst_ref=row_block(number, tok),
            send_sem=send1.at[number, step],
            recv_sem=recv1.at[number, step],
            device_id={"tok": target, "mdl": mdl},
        )

    def passed(number, step):
        block = row_block(number, source_at(step) * 2 + core)
        return pltpu.make_async_remote_copy(
            src_ref=block,
            dst_ref=block,
            send_sem=send2.at[number, step],
            recv_sem=recv2.at[number, step],
            device_id={"tok": sibling, "mdl": mdl},
        )

    def relayed(number, step):
        half = rows_in[number].shape[0] // 2
        first = (source_at(step) * 2 + core) * 2 * half + (step - 1) * half
        block = rows_out[number].at[pl.ds(pl.multiple_of(first, half), half), :]
        return pltpu.make_async_remote_copy(
            src_ref=block,
            dst_ref=block,
            send_sem=send3.at[number, step],
            recv_sem=recv3.at[number, step],
            device_id={"tok": chip_at(3 - step) * 2 + core, "mdl": mdl},
        )

    directs = (1, 2) if square else range(1, chips)

    def rightward(number, step):
        block = col_block(number, mdl - step)
        return pltpu.make_async_remote_copy(
            src_ref=block if step else cols_in[number],
            dst_ref=block,
            send_sem=to_right.at[number, step],
            recv_sem=from_left.at[number, step],
            device_id={"tok": tok, "mdl": mdl + 1},
        )

    def leftward(number, step):
        block = col_block(number, mdl + step)
        return pltpu.make_async_remote_copy(
            src_ref=block if step else cols_in[number],
            dst_ref=block,
            send_sem=to_left.at[number, step],
            recv_sem=from_right.at[number, step],
            device_id={"tok": tok, "mdl": mdl - 1},
        )

    def right_if(step):
        return (mdl >= step) & (mdl < n_mdl - 1)

    def left_if(step):
        return (mdl + step < n_mdl) & (mdl > 0)

    for number in range(n_col):
        @pl.when(right_if(0))
        def _():
            rightward(number, 0).start()

        @pl.when(left_if(0))
        def _():
            leftward(number, 0).start()

    locals_ = []
    for number in range(n_col):
        locals_.append(
            pltpu.make_async_copy(
                cols_in[number], col_block(number, mdl), local_sem.at[n_row + number]
            )
        )
        locals_[-1].start()
    for number in range(n_row):
        if prepare is not None:
            prepare(number)
        for step in directs:
            direct(number, step).start()
        direct(number, 0).start()
        locals_.append(
            pltpu.make_async_copy(rows_in[number], row_block(number, tok), local_sem.at[number])
        )
        locals_[-1].start()

    def finish_diagonal(number):
        for step in (1, 2):
            relayed(number, step).wait_recv()
        passed(number, 3).start()

    for turn in range(max(n_row, n_mdl - 2 if n_col else 0)):
        hop = turn + 1
        if hop < n_mdl - 1:
            for number in range(n_col):
                @pl.when(mdl >= hop)
                def _():
                    rightward(number, hop - 1).wait_recv()

                @pl.when(right_if(hop))
                def _():
                    rightward(number, hop).start()

                @pl.when(mdl + hop < n_mdl)
                def _():
                    leftward(number, hop - 1).wait_recv()

                @pl.when(left_if(hop))
                def _():
                    leftward(number, hop).start()

        if turn < n_row:
            for step in directs:
                direct(turn, step).wait_recv()
                if square:
                    relayed(turn, step).start()
                passed(turn, step).start()
            if square and turn > 0:
                finish_diagonal(turn - 1)
        if between is not None:
            between(turn)

    if square and n_row:
        finish_diagonal(n_row - 1)
    for copy in locals_:
        copy.wait()
    for number in range(n_col):
        @pl.when(mdl >= n_mdl - 1)
        def _():
            rightward(number, n_mdl - 2).wait_recv()

        @pl.when(mdl + n_mdl - 1 < n_mdl)
        def _():
            leftward(number, n_mdl - 2).wait_recv()

    for number in range(n_row):
        direct(number, 0).wait()
        for step in directs:
            direct(number, step).wait_send()
            if square:
                relayed(number, step).wait_send()
        for step in range(1, chips):
            passed(number, step).wait()
    for number in range(n_col):
        for step in range(n_mdl - 1):
            @pl.when(right_if(step))
            def _():
                rightward(number, step).wait_send()

            @pl.when(left_if(step))
            def _():
                leftward(number, step).wait_send()


def exchange_semaphores(n_tok, n_mdl, n_row, n_col):
    row_sem = pltpu.SemaphoreType.DMA((max(n_row, 1), n_tok // 2))
    col_sem = pltpu.SemaphoreType.DMA((max(n_col, 1), n_mdl))
    return [pltpu.SemaphoreType.DMA((n_row + n_col,))] + [row_sem] * 6 + [col_sem] * 4


def project_kernel(n_tok, n_mdl, head_width, *refs):
    normed, key_w, value_w, query_w, key_gain, query_gain, cosine, sine = refs[:8]
    keys_out, values_out, query_out = refs[8:11]
    keys, values, query, key_held, value_held, query_held, load_sem = refs[11:18]
    width = keys.shape[1]
    lanes = 2 * head_width
    block = 256 if width % 256 == 0 else lanes
    loads = [
        pltpu.make_async_copy(source, held, load_sem.at[number])
        for number, (source, held) in enumerate(
            ((key_w, key_held), (value_w, value_held), (query_w, query_held))
        )
    ]
    for load in loads:
        load.start()
    lane = lax.broadcasted_iota(jnp.int32, (1, lanes), 1)
    first = lane < head_width
    early = lane % head_width < head_width // 2

    def head_mean(terms):
        one = jnp.sum(jnp.where(first, terms, 0.0), axis=1, keepdims=True)
        other = jnp.sum(jnp.where(first, 0.0, terms), axis=1, keepdims=True)
        return jnp.where(first, one, other) * (1.0 / head_width)

    def finished(summed, gain):
        center = summed - head_mean(summed)
        normal = center * lax.rsqrt(head_mean(center * center) + 1e-06) * gain[...]
        partner = jnp.where(
            early,
            pltpu.roll(normal, lanes - head_width // 2, axis=1),
            pltpu.roll(normal, head_width // 2, axis=1),
        )
        return normal * cosine[...] + partner * sine[...]

    def project(held, gain, target):
        def step(number, carry):
            columns = pl.ds(pl.multiple_of(number * block, block), block)
            summed = jnp.dot(
                normed[...], held[:, columns], preferred_element_type=jnp.float32
            )
            if gain is not None:
                summed = jnp.concatenate(
                    [
                        finished(summed[:, start : start + lanes], gain)
                        for start in range(0, block, lanes)
                    ],
                    axis=1,
                )
            target[:, columns] = summed.astype(jnp.bfloat16)
            return carry

        lax.fori_loop(0, width // block, step, 0)

    def prepare(number):
        loads[number].wait()
        if number == 0:
            project(key_held, key_gain, keys)
        else:
            project(value_held, None, values)

    query_copy = pltpu.make_async_copy(query, query_out, load_sem.at[3])

    def between(turn):
        if turn == 0:
            loads[2].wait()
            project(query_held, query_gain, query)
            query_copy.start()

    exchange(
        n_tok,
        n_mdl,
        (keys, values),
        (),
        (keys_out, values_out),
        (),
        refs[18:],
        prepare,
        between,
    )
    query_copy.wait()


def project_and_gather(mesh, normed, weights, gains, cosine, sine, head_width, collective_id):
    n_tok, n_mdl = mesh.shape["tok"], mesh.shape["mdl"]
    own_rows, depth = normed.shape
    width = weights[0].shape[1]
    full = jax.ShapeDtypeStruct((own_rows * n_tok, width), jnp.bfloat16)
    own = jax.ShapeDtypeStruct((own_rows, width), jnp.bfloat16)
    anywhere = pl.BlockSpec(memory_space=pl.ANY)
    inside = pl.BlockSpec(memory_space=pltpu.VMEM)
    return pl.pallas_call(
        functools.partial(project_kernel, n_tok, n_mdl, head_width),
        out_shape=[full, full, own],
        in_specs=[inside] + [anywhere] * 3 + [inside] * 4,
        out_specs=[anywhere] * 3,
        scratch_shapes=[pltpu.VMEM((own_rows, width), jnp.bfloat16)] * 3
        + [pltpu.VMEM((depth, width), jnp.bfloat16)] * 3
        + [pltpu.SemaphoreType.DMA((4,))]
        + exchange_semaphores(n_tok, n_mdl, 2, 0),
        compiler_params=pltpu.CompilerParams(
            collective_id=collective_id, has_side_effects=True, vmem_limit_bytes=48 * 2**20
        ),
        name="project_and_gather",
    )(normed, *weights, *gains, cosine, sine)


def gather_all(mesh, over_tok, over_mdl, collective_id):
    n_tok, n_mdl = mesh.shape["tok"], mesh.shape["mdl"]
    n_row, n_col = len(over_tok), len(over_mdl)
    shapes = [
        jax.ShapeDtypeStruct((one.shape[0] * n_tok, one.shape[1]), one.dtype) for one in over_tok
    ] + [jax.ShapeDtypeStruct((one.shape[0], one.shape[1] * n_mdl), one.dtype) for one in over_mdl]
    return pl.pallas_call(
        functools.partial(gather_kernel, n_tok, n_mdl, n_row, n_col),
        out_shape=shapes,
        in_specs=[pl.BlockSpec(memory_space=pl.ANY)] * (n_row + n_col),
        out_specs=[pl.BlockSpec(memory_space=pl.ANY)] * (n_row + n_col),
        scratch_shapes=exchange_semaphores(n_tok, n_mdl, n_row, n_col),
        compiler_params=pltpu.CompilerParams(collective_id=collective_id, has_side_effects=True),
        name=f"gather_{collective_id}",
    )(*over_tok, *over_mdl)


def attend_kernel(rows_at_once, keys_at_once, head_width, meta_ref, q_ref, k_ref, v_ref, o_ref):
    bound, first_row = meta_ref[0], meta_ref[1]
    own_rows, lanes = q_ref.shape
    count = k_ref.shape[0]
    chunks = count // keys_at_once
    per = lanes // head_width
    lane = lax.broadcasted_iota(jnp.int32, (1, lanes), 1) // head_width
    masks = [(lane == head).astype(jnp.float32) for head in range(per)]
    edge = bound // keys_at_once
    edge_start = pl.multiple_of(edge * keys_at_once, keys_at_once)
    edge_keys = edge_start + lax.broadcasted_iota(jnp.int32, (keys_at_once, 1), 0)

    for block in range(own_rows // rows_at_once):
        rows = pl.ds(block * rows_at_once, rows_at_once)
        start = first_row + block * rows_at_once
        row_ids = start + lax.broadcasted_iota(jnp.int32, (rows_at_once, 1), 0)

        def add_chunk(carry, keys, values):
            queries = q_ref[rows, :]
            result = []
            for head in range(per):
                mine = queries * (masks[head] * head_width ** (-0.5)).astype(jnp.bfloat16)
                score = lax.dot_general(
                    mine, keys, (((1,), (1,)), ((), ())), preferred_element_type=jnp.float32
                )
                expo = jnp.exp(score).astype(jnp.bfloat16)
                result.append(
                    carry[head]
                    + jnp.dot(expo, values[head], preferred_element_type=jnp.float32)
                )
            return tuple(result)

        def inner(chunk, carry):
            here = pl.ds(pl.multiple_of(chunk * keys_at_once, keys_at_once), keys_at_once)
            values = v_ref[here, :]
            with_ones = [
                values * mask.astype(jnp.bfloat16) + (1.0 - mask).astype(jnp.bfloat16)
                for mask in masks
            ]
            return add_chunk(carry, k_ref[here, :], with_ones)

        for request in range(2):
            active = start < bound if request == 0 else start + rows_at_once > bound

            @pl.when(active)
            def _():
                here = pl.ds(edge_start, keys_at_once)
                inside = edge_keys < bound if request == 0 else edge_keys >= bound
                wide = v_ref[here, :].astype(jnp.float32)
                with_ones = [
                    jnp.where(inside, wide * mask + (1.0 - mask), 0.0).astype(jnp.bfloat16)
                    for mask in masks
                ]
                zero = jnp.zeros((rows_at_once, lanes), jnp.float32)
                carry = add_chunk((zero,) * per, k_ref[here, :], with_ones)
                if request == 0:
                    low, high = 0, edge
                else:
                    low, high = edge + 1, chunks
                carry = lax.fori_loop(low, high, inner, carry)
                output = zero
                for head in range(per):
                    total = pltpu.roll(carry[head], head_width, axis=1)
                    output = jnp.where(lane == head, carry[head] / total, output)
                if request == 0:
                    o_ref[rows, :] = output.astype(o_ref.dtype)
                else:
                    old = o_ref[rows, :].astype(jnp.float32)
                    o_ref[rows, :] = jnp.where(row_ids >= bound, output, old).astype(o_ref.dtype)


def attend(query, keys, values, bound, first_row, head_width, part, parts):
    width = query.shape[1]
    own_rows = query.shape[0] // parts
    count = keys.shape[0]
    lanes = 2 * head_width
    meta = jnp.stack([bound, first_row + part * own_rows]).astype(jnp.int32)
    block = pl.BlockSpec((own_rows, lanes), lambda pair, meta: (part, pair))
    out_block = pl.BlockSpec((own_rows, lanes), lambda pair, meta: (0, pair))
    full = pl.BlockSpec((count, lanes), lambda pair, meta: (0, pair))
    return pl.pallas_call(
        functools.partial(attend_kernel, min(256, own_rows), 512, head_width),
        out_shape=jax.ShapeDtypeStruct((own_rows, width), jnp.bfloat16),
        grid_spec=pltpu.PrefetchScalarGridSpec(
            num_scalar_prefetch=1,
            grid=(width // lanes,),
            in_specs=[block, full, full],
            out_specs=out_block,
        ),
        compiler_params=pltpu.CompilerParams(vmem_limit_bytes=58 * 2**20),
        cost_estimate=pl.CostEstimate(
            flops=4 * own_rows * count * width,
            bytes_accessed=4 * count * width,
            transcendentals=own_rows * count * width // head_width,
        ),
        name=f"attend_{part}_{parts}",
    )(meta, query, keys, values)


def shards(
    mesh,
    hidden_states,
    lengths,
    positions,
    modulation,
    query_weight,
    key_weight,
    value_weight,
    out_weight,
    query_gain,
    key_gain,
):
    own_rows = hidden_states.shape[0]
    head_width = query_gain.shape[0]
    full_rows = lax.all_gather(hidden_states, "mdl", axis=1, tiled=True)
    key_full, value_full, query_full = gather_all(
        mesh, [key_weight, value_weight, query_weight], [], 0
    )
    row_index = lax.axis_index("tok") * own_rows + jnp.arange(own_rows, dtype=jnp.int32)
    request, is_text, bound = token_labels(row_index, lengths)
    normed = modulate(full_rows, modulation, is_text)
    angles = pair_angles(positions, head_width // 2)
    textual = is_text[:, None]
    cosine = jnp.tile(jnp.where(textual, 1.0, jnp.cos(angles)), (1, 4))
    sine = jnp.where(textual, 0.0, jnp.sin(angles))
    sine = jnp.tile(jnp.concatenate([-sine, sine], axis=1), (1, 2))
    keys, values, query_flat = project_and_gather(
        mesh,
        normed,
        (key_full, value_full, query_full),
        [jnp.tile(gain, 2)[None, :] for gain in (key_gain, query_gain)],
        cosine,
        sine,
        head_width,
        1,
    )
    first_row = lax.axis_index("tok") * own_rows
    early, middle, second = (
        attend(query_flat, keys, values, bound, first_row, head_width, part, parts)
        for part, parts in ((0, 4), (1, 4), (1, 2))
    )
    first_heads = jnp.concatenate(
        [lax.all_gather(piece, "mdl", axis=1, tiled=True) for piece in (early, middle)], axis=0
    )
    out_full, second_heads = gather_all(mesh, [out_weight], [second], 2)
    out_width = out_weight.shape[1]
    projected = jnp.concatenate(
        [
            jnp.dot(heads, out_full, preferred_element_type=jnp.float32)
            for heads in (first_heads, second_heads)
        ],
        axis=0,
    )
    gate_rows = lax.dynamic_slice_in_dim(
        modulation, lax.axis_index("mdl") * out_width, out_width, 1
    )
    gate = jnp.where(is_text[:, None], gate_rows[5][None, :], gate_rows[2][None, :])
    return (hidden_states.astype(jnp.float32) + gate * projected).astype(jnp.bfloat16)


def solution(mesh):
    return jax.shard_map(
        functools.partial(shards, mesh),
        mesh=mesh,
        in_specs=(
            P("tok", "mdl"),
            P(),
            P(None, "tok"),
            P(),
            P("tok", "mdl"),
            P("tok", "mdl"),
            P("tok", "mdl"),
            P("tok", "mdl"),
            P(),
            P(),
        ),
        out_specs=P("tok", "mdl"),
        check_vma=False,
    )
```
